32 devices in a mesh: img: 8 (over y, x, core), band: 4 (over z).
Axes of the slice: x: 2, y: 2, z: 4, core: 2. Of those that a mesh axis runs over, the one named last changes fastest.
Arguments:
- inputs: bfloat16 [32, 256, 768], P('img', 'band'), may hold values from -6 to 6
- keep_mask: int32 [32, 256], P('img', 'band'), may hold values 0 or 1
- crop_rows: int32 [32], P('img'), may hold values from 12 to 16
- crop_cols: int32 [32], P('img'), may hold values from 12 to 16
- gain_one: bfloat16 [768], replicated, may hold values from 0.5 to 1.5
- shift_one: bfloat16 [768], replicated, may hold values from -3 to 3
- w_query: bfloat16 [768, 768], replicated, may hold values from -0.3125 to 0.3125
- b_query: bfloat16 [768], replicated, may hold values from -3 to 3
- w_key: bfloat16 [768, 768], replicated, may hold values from -0.3125 to 0.3125
- w_value: bfloat16 [768, 768], replicated, may hold values from -0.21875 to 0.21875
- b_value: bfloat16 [768], replicated, may hold values from -3 to 3
- w_out: bfloat16 [768, 768], replicated, may hold values from -0.875 to 0.875
- b_out: bfloat16 [768], replicated, may hold values from -3 to 3
- gain_two: bfloat16 [768], replicated, may hold values from 0.5 to 1.5
- shift_two: bfloat16 [768], replicated, may hold values from -3 to 3
- w_up: bfloat16 [768, 3072], replicated, may hold values from -0.21875 to 0.21875
- b_up: bfloat16 [3072], replicated, may hold values from -3 to 3
- w_down: bfloat16 [3072, 768], replicated, may hold values from -0.109375 to 0.109375
- b_down: bfloat16 [768], replicated, may hold values from -3 to 3
- cotangent: bfloat16 [32, 256, 768], P('img', 'band'), may hold values from -6 to 6
Outputs:
- output: bfloat16 [32, 256, 768], P('img', 'band')
- grad_inputs: float32 [32, 256, 768], P('img', 'band')
- grad_gain_one: float32 [768], P(('img', 'band'))
- grad_shift_one: float32 [768], P(('img', 'band'))
- grad_w_query: float32 [768, 768], P(('img', 'band'))
- grad_b_query: float32 [768], P(('img', 'band'))
- grad_w_key: float32 [768, 768], P(('img', 'band'))
- grad_w_value: float32 [768, 768], P(('img', 'band'))
- grad_b_value: float32 [768], P(('img', 'band'))
- grad_w_out: float32 [768, 768], P(('img', 'band'))
- grad_b_out: float32 [768], P(('img', 'band'))
- grad_gain_two: float32 [768], P(('img', 'band'))
- grad_shift_two: float32 [768], P(('img', 'band'))
- grad_w_up: float32 [768, 3072], P(('img', 'band'))
- grad_b_up: float32 [3072], P(('img', 'band'))
- grad_w_down: float32 [3072, 768], P(('img', 'band'))
- grad_b_down: float32 [768], P(('img', 'band'))
The draws below stay inside these ranges and needn't reach their ends.
Inputs may be any that keep to these rules, and one draw needn't show every extreme that they name: Grid rows 0 to crop_rows[i] - 1 of image i lie in its crop. Grid columns 0 to crop_cols[i] - 1 of image i lie in its crop.
All inputs are finite; a program needn't handle non-finite values. No bound on the sum of `keep_mask` on one device may be relied on, other than what follows from the above.
Results may differ from the reference program's by a relative error of at most 0.015.
The reference program's roundings to bfloat16 on the way count: a program that leaves them out, or rounds other values in their place, can miss the bound.
Values may be sent and summed in bfloat16 or wider, within the bound.
No kernel may reach another device: no remote copies, remote signals or barrier semaphores. Data moves between devices by JAX's collectives and lax.ppermute only.
A program may use at most 128 MiB of HBM per device.

```python
import math
import jax
import jax.numpy as jnp
from jax import lax

D = 768
HEADS = 16
HEAD_DIM = 48
FF = 3072
SIDE = 16
GRID = 256
IMAGES = 32


def set_ends(values, stream_key, low, high):
    place = [jax.random.randint(jax.random.fold_in(stream_key, axis), (), 0, length) for axis, length in enumerate(values.shape)]
    longest = values.shape.index(max(values.shape))
    beside = place[:longest] + [(place[longest] + 1) % values.shape[longest]] + place[longest + 1:]
    return values.at[tuple(place)].set(low).at[tuple(beside)].set(high)


def with_spikes(values, rng, source, target, shards_of, factor):
    def block_of(axis_at):
        return (jnp.arange(values.shape[axis_at]) // (values.shape[axis_at] // shards_of)).reshape((-1,) + (1,) * (values.ndim - 1 - axis_at))

    first = jax.random.permutation(rng, shards_of)[block_of(target)]
    other_side = (block_of(target) + shards_of // 2) % shards_of
    return jnp.where((block_of(source) == first) | (block_of(source) == other_side), factor * values, values)


def levels(own_key, extent, split, least, high):
    level = 1.0
    for dim, parts in split:
        draws = jax.random.uniform(jax.random.fold_in(jax.random.fold_in(own_key, 6), dim), (parts,), jnp.float32, least / len(split), high / len(split))
        level = level * jnp.repeat(jnp.exp(draws), extent[dim] // parts).reshape((-1,) + (1,) * (len(extent) - 1 - dim))
    return level


def normal_values(own_key, shape, deviation, bound, cuts=(), kind=jnp.bfloat16):
    array = jax.random.normal(own_key, shape, jnp.float32) * deviation
    if len(cuts) > 0:
        array = levels(own_key, shape, cuts, -0.22, 0.18) * array
    return jnp.clip(array, min=-bound, max=bound).astype(kind)


def gaussian_with(rng, dims, deviation, limit, shards, heavy, held_as=jnp.bfloat16):
    drawn = deviation * jax.random.normal(rng, dims, jnp.float32)
    if shards:
        drawn = drawn * levels(rng, dims, shards, -0.22, 0.18)
    return jnp.clip(with_spikes(drawn, jax.random.fold_in(rng, 3), *heavy), -limit, limit).astype(held_as)


def setup_inputs(seed: int = 0) -> dict:
    key_list = jax.random.split(jax.random.key(seed), 21)
    return {
        "inputs": normal_values(key_list[0], (IMAGES, GRID, D), 1.0, 6.0, ((0, 8), (1, 4))),
        "keep_mask": set_ends((jax.random.randint(key_list[1], (IMAGES, GRID), 0, 8) < 7).astype(jnp.int32), jax.random.fold_in(key_list[1], 1), 0, 1),
        "crop_rows": set_ends(jax.random.randint(key_list[2], (IMAGES,), 3 * SIDE // 4, SIDE + 1), jax.random.fold_in(key_list[2], 1), 3 * SIDE // 4, SIDE).astype(jnp.int32),
        "crop_cols": set_ends(jax.random.randint(key_list[3], (IMAGES,), 3 * SIDE // 4, SIDE + 1), jax.random.fold_in(key_list[3], 1), 3 * SIDE // 4, SIDE).astype(jnp.int32),
        "gain_one": jnp.clip(1.0 + 0.1 * jax.random.normal(key_list[4], (D,), jnp.float32), 0.5, 1.5).astype(jnp.bfloat16),
        "shift_one": normal_values(key_list[5], (D,), 0.3, 3.0),
        "w_query": normal_values(key_list[6], (D, D), (D // 2) ** -0.5, 0.3125),
        "b_query": normal_values(key_list[7], (D,), 0.5, 3.0),
        "w_key": normal_values(key_list[8], (D, D), (D // 2) ** -0.5, 0.3125),
        "w_value": normal_values(key_list[9], (D, D), D ** -0.5, 0.21875),
        "b_value": normal_values(key_list[10], (D,), 0.5, 3.0),
        "w_out": normal_values(key_list[11], (D, D), (D // 16) ** -0.5, 0.875),
        "b_out": normal_values(key_list[12], (D,), 0.3, 3.0),
        "gain_two": jnp.clip(1.0 + 0.1 * jax.random.normal(key_list[13], (D,), jnp.float32), 0.5, 1.5).astype(jnp.bfloat16),
        "shift_two": normal_values(key_list[14], (D,), 0.3, 3.0),
        "w_up": normal_values(key_list[15], (D, FF), D ** -0.5, 0.21875),
        "b_up": normal_values(key_list[16], (FF,), 0.5, 3.0),
        "w_down": normal_values(key_list[17], (FF, D), FF ** -0.5, 0.109375),
        "b_down": normal_values(key_list[18], (D,), 0.3, 3.0),
        "cotangent": gaussian_with(key_list[19], (IMAGES, GRID, D), 1.0, 6.0, ((0, 8), (1, 4)), (0, 2, 8, 2.0)),
    }


@jax.custom_vjp
def low(v):
    return lax.optimization_barrier(v.astype(jnp.bfloat16)).astype(jnp.float32)

@jax.custom_vjp
def low_back(v):
    return v

def low_keep(v):
    return (low(v), None)

def low_pass(kept, grad):
    return (grad,)

def back_keep(v):
    return (v, None)

def back_low(kept, grad):
    return (low(grad),)
low.defvjp(low_keep, low_pass)
low_back.defvjp(back_keep, back_low)
highest = lax.Precision.HIGHEST
epsilon = 1e-05

def normalize(tensor, gain_vector, shift_vector):
    average = lax.optimization_barrier(jnp.mean(tensor, axis=-1, keepdims=True))
    centred = tensor - average
    variance = lax.optimization_barrier(jnp.mean(centred * centred, axis=-1, keepdims=True))
    return centred * lax.rsqrt(variance + epsilon) * gain_vector + shift_vector

def project(tensor, matrix):
    return jnp.einsum('ngd,de->nge', tensor, matrix, precision=highest)

def forward(block_inputs, group_valid, weights):
    gain_one, shift_one, w_query, b_query, w_key, w_value, b_value, w_out, b_out, gain_two, shift_two, w_up, b_up, w_down, b_down = weights
    image_count = block_inputs.shape[0]
    normed = low(normalize(block_inputs, gain_one, shift_one))
    queries = low(low_back(project(normed, w_query) + b_query))
    keys_all = low(low_back(project(normed, w_key)))
    values_all = low(low_back(project(normed, w_value) + b_value))
    shape_heads = (image_count, GRID, HEADS, HEAD_DIM)
    scores = jnp.einsum('bqhe,bkhe->bhqk', queries.reshape(shape_heads), keys_all.reshape(shape_heads), precision=highest) * HEAD_DIM ** (-0.5)
    scores = jnp.where(group_valid[:, None, None, :] > 0.5, scores, -1e+30)
    scores = low_back(scores)
    probability = low(jax.nn.softmax(scores, axis=-1))
    mixed_heads = jnp.einsum('bhqk,bkhe->bqhe', probability, values_all.reshape(shape_heads), precision=highest)
    attended = low(low_back(mixed_heads.reshape(image_count, GRID, D)))
    branch = low_back(project(attended, w_out) + b_out)
    middle = block_inputs + branch
    normed_two = low(normalize(middle, gain_two, shift_two))
    hidden = low_back(project(normed_two, w_up) + b_up)
    activated = low(jax.nn.gelu(hidden, approximate=False))
    down_out = low_back(project(activated, w_down) + b_down)
    return group_valid[:, :, None] * (middle + down_out)

def reference(inputs, keep_mask, crop_rows, crop_cols, gain_one, shift_one, w_query, b_query, w_key, w_value, b_value, w_out, b_out, gain_two, shift_two, w_up, b_up, w_down, b_down, cotangent):
    position = jnp.arange(GRID, dtype=jnp.int32)
    inside = (keep_mask > 0) & (position[None, :] // SIDE < crop_rows[:, None]) & (position[None, :] % SIDE < crop_cols[:, None])
    validity = inside.astype(jnp.float32)
    parameters = tuple((weight.astype(jnp.float32) for weight in (gain_one, shift_one, w_query, b_query, w_key, w_value, b_value, w_out, b_out, gain_two, shift_two, w_up, b_up, w_down, b_down)))
    per_group = math.gcd(IMAGES, 16)
    group_count = IMAGES // per_group

    def scan_step(running_sums, pieces):
        group_inputs, group_valid, group_cotangent = pieces

        def forward_part(block_inputs, weights):
            return forward(block_inputs, group_valid, weights)
        result, pullback = jax.vjp(forward_part, group_inputs, parameters)
        gradients = pullback(group_cotangent)
        running_sums = jax.tree.map(lambda running, addend: running + addend, running_sums, gradients[1])
        return (running_sums, (result, gradients[0]))
    zeros_start = tuple((jnp.zeros_like(weight) for weight in parameters))
    sums, (results, grad_inputs) = lax.scan(scan_step, zeros_start, (inputs.astype(jnp.float32).reshape(group_count, per_group, GRID, D), validity.reshape(group_count, per_group, GRID), cotangent.astype(jnp.float32).reshape(group_count, per_group, GRID, D)))
    return (results.reshape(IMAGES, GRID, D).astype(jnp.bfloat16), grad_inputs.reshape(IMAGES, GRID, D), sums[0], sums[1], sums[2], sums[3], sums[4], sums[5], sums[6], sums[7], sums[8], sums[9], sums[10], sums[11], sums[12], sums[13], sums[14])
```

```python
import jax
import jax.numpy as jnp
from jax import lax
from jax.sharding import PartitionSpec as P

HEADS = 16
HEAD_DIM = 48
SIDE = 16
EPS = 1e-05
F32 = jnp.float32
BF16 = jnp.bfloat16


def dot_nn(a, b):
    return lax.dot_general(a, b, (((1,), (0,)), ((), ())), preferred_element_type=F32)


def dot_nt(a, b):
    return lax.dot_general(a, b, (((1,), (1,)), ((), ())), preferred_element_type=F32)


def dot_tn(a, b):
    return lax.dot_general(a, b, (((0,), (0,)), ((), ())), preferred_element_type=F32)


def norm_stats(x):
    mean = jnp.mean(x, axis=-1, keepdims=True)
    centred = x - mean
    var = jnp.mean(centred * centred, axis=-1, keepdims=True)
    r = lax.rsqrt(var + EPS)
    return centred * r, r


def norm_back(grad, n, r, gain):
    e = grad * gain
    return r * (e - jnp.mean(e, axis=-1, keepdims=True) - n * jnp.mean(e * n, axis=-1, keepdims=True))


def colsum(x):
    return jnp.sum(x.astype(F32), axis=0)


def take(x, index, axis):
    return lax.dynamic_index_in_dim(x, index, axis, keepdims=False)


class Links:
    def __init__(self, n_img, n_band):
        self.n_img, self.nb = n_img, n_band
        self.hi = n_img // 8
        i = lax.axis_index("img")
        self.c = i & 1
        self.p = (i >> 1) & 1
        self.q = (i >> 2) & 1
        self.h = i >> 3
        self.b = lax.axis_index("band")

    def flip(self, x, bit):
        return lax.ppermute(x, "img", [(k, k ^ bit) for k in range(self.n_img)])

    def band_shift(self, x, s):
        return lax.ppermute(x, "band", [(k, (k + s) % self.nb) for k in range(self.nb)])

    def hi_shift(self, x, s):
        n = self.n_img
        return lax.ppermute(x, "img", [(k, (k + 8 * s) % n) for k in range(n)])

    def scatter_in(self, x):
        slots = [take(x, self.b, 0)]
        for s in range(1, self.nb):
            blk = take(x, (self.b + s) % self.nb, 0)
            slots.append(self.band_shift(blk, s))
        return slots

    def scatter_back(self, slots):
        got = [slots[0]]
        for s in range(1, self.nb):
            got.append(self.band_shift(slots[s], -s))
        stacked = jnp.stack(got + got)
        return lax.dynamic_slice_in_dim(stacked, (self.nb - self.b) % self.nb, self.nb, axis=0)

    def reduce(self, grad, k, wire=BF16):
        rows, cols = grad.shape
        hi, nb = self.hi, self.nb
        R = rows // (hi * 4 * k * nb)
        half = cols // 2
        g = grad.astype(wire).reshape(hi, 2, 2, k * nb * R, cols)
        a, b = g[..., :half], g[..., half:]
        a_r = self.flip(take(a, 1 - self.p, 2), 2)
        b_r = self.flip(take(b, 1 - self.q, 1), 4)
        a_k = take(a, self.p, 2)
        b_k = take(b, self.q, 1)

        def add(*xs):
            t = xs[0].astype(F32)
            for x in xs[1:]:
                t = t + x.astype(F32)
            return t

        a_s = add(take(a_k, 1 - self.q, 1), take(a_r, 1 - self.q, 1)).astype(wire)
        b_s = add(take(b_k, 1 - self.p, 1), take(b_r, 1 - self.p, 1)).astype(wire)
        a_r2 = self.flip(a_s, 4)
        b_r2 = self.flip(b_s, 2)
        a2 = add(take(a_k, self.q, 1), take(a_r, self.q, 1), a_r2)
        b2 = add(take(b_k, self.p, 1), take(b_r, self.p, 1), b_r2)
        held = jnp.concatenate([a2, b2], axis=-1)
        if hi > 1:
            total = take(held, self.h, 0)
            for s in range(1, hi):
                total = total + self.hi_shift(take(held, (self.h + s) % hi, 0).astype(wire), s).astype(F32)
            held = total
        else:
            held = held[0]
        held = held.reshape(k, nb, R, cols)
        low = held.astype(wire)
        total = take(held, self.b, 1)
        for s in range(1, nb):
            total = total + self.band_shift(take(low, (self.b + s) % nb, 1), s).astype(F32)
        return total

    def rows_unit(self, left, right):
        tokens, width = left.shape
        split = left.reshape(tokens, self.hi * 4, 2, width // (self.hi * 8))
        keep = take(split, self.c, 2).reshape(tokens, width // 2)
        send = take(split, 1 - self.c, 2).reshape(tokens, width // 2)
        got = self.flip(jnp.concatenate([send, right], axis=1), 1)
        grad = dot_tn(keep, right) + dot_tn(got[:, : width // 2], got[:, width // 2 :])
        return self.reduce(grad, 1)[0]

    def cols_unit(self, left, rights):
        width = left.shape[1]
        halves = [r.shape[1] // 2 for r in rights]
        mine = jnp.concatenate(
            [lax.dynamic_slice_in_dim(r, self.c * h, h, 1) for r, h in zip(rights, halves)], axis=1
        )
        send = jnp.concatenate(
            [lax.dynamic_slice_in_dim(r, (1 - self.c) * h, h, 1) for r, h in zip(rights, halves)], axis=1
        )
        got = self.flip(jnp.concatenate([left, send], axis=1), 1)
        grad = dot_tn(left, mine) + dot_tn(got[:, :width], got[:, width:])
        done = self.reduce(grad, 2)
        own, other = take(done, self.c, 0), self.flip(take(done, 1 - self.c, 0), 1)
        outs, at = [], 0
        for h in halves:
            x, y = own[:, at : at + h], other[:, at : at + h]
            at += h
            outs.append(jnp.concatenate([jnp.where(self.c == 0, x, y), jnp.where(self.c == 0, y, x)], axis=1))
        return outs

    def small_unit(self, vectors):
        n = self.n_img * self.nb
        packed = jnp.concatenate([v.reshape(n, -1) for v in vectors], axis=1)
        width = packed.shape[1]
        pad = -width % 256
        packed = jnp.pad(packed, ((0, 0), (0, pad)))
        width += pad
        g = packed.reshape(self.hi * 4, 2, self.nb, width)
        g = take(g, self.c, 1) + self.flip(take(g, 1 - self.c, 1), 1)
        done = self.reduce(g.reshape(-1, width), 1, F32)[0, 0]
        outs, at = [], 0
        for v in vectors:
            size = v.shape[0] // n
            outs.append(done[at : at + size])
            at += size
        return outs


def gelu_parts(u):
    cdf = 0.5 * (1.0 + lax.erf(u * 0.7071067811865476))
    pdf = jnp.exp(-0.5 * u * u) * 0.3989422804014327
    return cdf, pdf


def per_device(
    inputs, keep_mask, crop_rows, crop_cols, gain_one, shift_one, w_query, b_query, w_key, w_value,
    b_value, w_out, b_out, gain_two, shift_two, w_up, b_up, w_down, b_down, cotangent, *, n_img, nb,
):
    images, rows, width = inputs.shape
    own = images // nb
    links = Links(n_img, nb)
    f = lambda v: v.astype(F32)
    position = links.b * rows + jnp.arange(rows, dtype=jnp.int32)
    inside = (
        (keep_mask > 0)
        & (position[None, :] // SIDE < crop_rows[:, None])
        & (position[None, :] % SIDE < crop_cols[:, None])
    )
    flags = inside.astype(BF16)
    flag_rows = jnp.pad(flags[:, None, :], ((0, 0), (0, 7), (0, width - rows)))
    packed = jnp.concatenate([inputs, flag_rows], axis=1).reshape(nb, own, rows + 8, width)
    slots = links.scatter_in(packed)
    cot_slots = links.scatter_in(cotangent.reshape(nb, own, rows, width))
    x = jnp.stack([s[:, :rows] for s in slots], axis=1)
    count = nb * rows
    tokens = own * count
    x = x.reshape(tokens, width).astype(F32)
    valid = jnp.stack([s[:, rows, :rows] for s in slots], axis=1).reshape(own, count).astype(F32)
    flat_valid = valid.reshape(tokens, 1)
    cot = jnp.stack(cot_slots, axis=1).reshape(tokens, width)

    n1, r1 = norm_stats(x)
    normed = (n1 * f(gain_one) + f(shift_one)).astype(BF16)
    q = (dot_nn(normed, w_query) + f(b_query)).astype(BF16)
    k = dot_nn(normed, w_key).astype(BF16)
    v = (dot_nn(normed, w_value) + f(b_value)).astype(BF16)
    heads = (own, count, HEADS, HEAD_DIM)
    qh, kh, vh = q.reshape(heads), k.reshape(heads), v.reshape(heads)
    scale = HEAD_DIM ** (-0.5)
    scores = jnp.einsum("bqhe,bkhe->bhqk", qh, kh, preferred_element_type=F32) * scale
    scores = jnp.where(valid[:, None, None, :] > 0.5, scores, -1e30)
    top = jnp.max(scores, axis=-1, keepdims=True)
    expd = jnp.exp(scores - top)
    prob = expd / jnp.sum(expd, axis=-1, keepdims=True)
    prob_low = prob.astype(BF16)
    attended = (
        jnp.einsum("bhqk,bkhe->bqhe", prob_low, vh, preferred_element_type=F32)
        .astype(BF16)
        .reshape(tokens, width)
    )
    middle = x + (dot_nn(attended, w_out) + f(b_out))
    n2, r2 = norm_stats(middle)
    normed_two = (n2 * f(gain_two) + f(shift_two)).astype(BF16)
    hidden = dot_nn(normed_two, w_up) + f(b_up)
    cdf, pdf = gelu_parts(hidden)
    activated = (hidden * cdf).astype(BF16)
    grad_result = cot.astype(F32) * flat_valid
    grad_down = grad_result.astype(BF16)
    g_w_down = links.rows_unit(activated, grad_down)
    out_full = (flat_valid * (middle + (dot_nn(activated, w_down) + f(b_down)))).astype(BF16)
    output = links.scatter_back(list(jnp.moveaxis(out_full.reshape(own, nb, rows, width), 1, 0)))
    grad_hidden = (dot_nt(grad_down, w_down) * (cdf + hidden * pdf)).astype(BF16)
    (g_w_up,) = links.cols_unit(normed_two, [grad_hidden])
    grad_norm_two = dot_nt(grad_hidden, w_up)
    grad_middle = grad_result + norm_back(grad_norm_two, n2, r2, f(gain_two))
    grad_branch = grad_middle.astype(BF16)
    (g_w_out,) = links.cols_unit(attended, [grad_branch])
    gah = dot_nt(grad_branch, w_out).astype(BF16).reshape(heads)
    grad_prob = jnp.einsum("bqhe,bkhe->bhqk", gah, vh, preferred_element_type=F32)
    delta = jnp.sum(prob * grad_prob, axis=-1, keepdims=True)
    grad_scores = (prob * (grad_prob - delta)).astype(BF16)
    gq = (jnp.einsum("bhqk,bkhe->bqhe", grad_scores, kh, preferred_element_type=F32) * scale).astype(BF16)
    gk = (jnp.einsum("bhqk,bqhe->bkhe", grad_scores, qh, preferred_element_type=F32) * scale).astype(BF16)
    gv = jnp.einsum("bhqk,bqhe->bkhe", prob_low, gah, preferred_element_type=F32).astype(BF16)
    gq, gk, gv = (t.reshape(tokens, width) for t in (gq, gk, gv))
    g_w_query, g_w_key, g_w_value = links.cols_unit(normed, [gq, gk, gv])
    grad_normed = dot_nt(gq, w_query) + dot_nt(gk, w_key) + dot_nt(gv, w_value)
    grad_x = grad_middle + norm_back(grad_normed, n1, r1, f(gain_one))
    back = links.scatter_back(
        list(jnp.moveaxis(grad_x.astype(BF16).reshape(own, nb, rows, width), 1, 0))
    )
    smalls = links.small_unit(
        [
            jnp.sum(grad_normed * n1, axis=0),
            jnp.sum(grad_normed, axis=0),
            colsum(gq),
            colsum(gv),
            colsum(grad_branch),
            jnp.sum(grad_norm_two * n2, axis=0),
            jnp.sum(grad_norm_two, axis=0),
            colsum(grad_hidden),
            colsum(grad_down),
        ]
    )
    return (
        output.reshape(inputs.shape),
        back.astype(F32).reshape(inputs.shape),
        smalls[0],
        smalls[1],
        g_w_query,
        smalls[2],
        g_w_key,
        g_w_value,
        smalls[3],
        g_w_out,
        smalls[4],
        smalls[5],
        smalls[6],
        g_w_up,
        smalls[7],
        g_w_down,
        smalls[8],
    )


def solution(mesh):
    n_img, nb = mesh.shape["img"], mesh.shape["band"]

    def body(*args):
        return per_device(*args, n_img=n_img, nb=nb)

    both = P(("img", "band"))
    rows = P(("img", "band"), None)
    token = P("img", "band", None)
    return jax.shard_map(
        body,
        mesh=mesh,
        in_specs=(token, P("img", "band"), P("img"), P("img")) + (P(),) * 15 + (token,),
        out_specs=(
            token, token, both, both, rows, both, rows, rows, both, rows, both, both, both, rows, both,
            rows, both,
        ),
        check_vma=False,
    )
```

```python
import functools

import jax
import jax.numpy as jnp
from jax import lax
from jax.experimental import pallas as pl
from jax.experimental.pallas import tpu as pltpu
from jax.sharding import PartitionSpec as P

HEADS = 16
HEAD_DIM = 48
SIDE = 16
EPS = 1e-05
F32 = jnp.float32
BF16 = jnp.bfloat16
GROUP = 8
GROUP_LANES = GROUP * HEAD_DIM
SCALE = HEAD_DIM ** (-0.5)


def dot_nn(a, b):
    return lax.dot_general(a, b, (((1,), (0,)), ((), ())), preferred_element_type=F32)


def dot_nt(a, b):
    return lax.dot_general(a, b, (((1,), (1,)), ((), ())), preferred_element_type=F32)


def dot_tn(a, b):
    return lax.dot_general(a, b, (((0,), (0,)), ((), ())), preferred_element_type=F32)


def norm_stats(x):
    mean = jnp.mean(x, axis=-1, keepdims=True)
    centred = x - mean
    var = jnp.mean(centred * centred, axis=-1, keepdims=True)
    r = lax.rsqrt(var + EPS)
    return centred * r, r


def norm_back(grad, n, r, gain):
    e = grad * gain
    return r * (e - jnp.mean(e, axis=-1, keepdims=True) - n * jnp.mean(e * n, axis=-1, keepdims=True))


def colsum(x):
    return jnp.sum(x.astype(F32), axis=0, keepdims=True)


def take(x, index, axis):
    return lax.dynamic_index_in_dim(x, index, axis, keepdims=False)


GAIN1, SHIFT1, BQ, BV, BO, GAIN2, SHIFT2, BDOWN = range(8)


def windows():
    out = []
    for h in range(GROUP):
        first, last = h * HEAD_DIM, (h + 1) * HEAD_DIM
        lo, hi = first // 128 * 128, -(-last // 128) * 128
        out.append((lo, hi, first - lo, last - lo))
    return out


def head_lanes(shape, first, last):
    lane = lax.broadcasted_iota(jnp.int32, shape, 1)
    return (lane >= first) & (lane < last)


def turn(x):
    return jnp.transpose(x.astype(F32)).astype(BF16)


def join(refs, rows):
    return jnp.concatenate([r[:rows, :] for r in refs], axis=0)


def column_of(row):
    n = row.shape[1]
    eye = lax.broadcasted_iota(jnp.int32, (n, n), 0) == lax.broadcasted_iota(jnp.int32, (n, n), 1)
    return jnp.sum(jnp.where(eye, row, 0.0), axis=1, keepdims=True)


def attend_kernel(rows, nb, *refs):
    slots = refs[:nb]
    vec, wq, wk, wv, wo = refs[nb : nb + 5]
    normed_t, q_o, k_o, v_o, att_t, mid_o, two_o, two_t, mask_o, att_o, kt = refs[nb + 5 :]
    tokens = nb * rows
    row = jnp.zeros((1, tokens), F32)
    for s in range(nb):
        row = row + slots[s][rows : rows + 8, :tokens].astype(F32)[s : s + 1, :]
    mask_o[...] = jnp.broadcast_to(row, mask_o.shape)
    x = join(slots, rows).astype(F32)
    n1, _ = norm_stats(x)
    normed = (n1 * vec[GAIN1 : GAIN1 + 1, :] + vec[SHIFT1 : SHIFT1 + 1, :]).astype(BF16)
    normed_t[...] = turn(normed)
    q_o[...] = (dot_nn(normed, wq[...]) + vec[BQ : BQ + 1, :]).astype(BF16)
    k = dot_nn(normed, wk[...]).astype(BF16)
    k_o[...] = k
    kt[...] = turn(k)
    v_o[...] = (dot_nn(normed, wv[...]) + vec[BV : BV + 1, :]).astype(BF16)
    keep = row > 0.5

    def group(g, carry):
        base = pl.multiple_of(g * GROUP_LANES, 128)
        blocks = [jnp.zeros((tokens, 128), F32) for _ in range(GROUP_LANES // 128)]
        for lo, hi, first, last in windows():
            wide = hi - lo
            here = head_lanes((tokens, wide), first, last)
            at = pl.ds(base + lo, wide)
            zero = jnp.zeros((tokens, wide), BF16)
            qm = jnp.where(here, q_o[:, at], zero)
            s = dot_nn(qm, kt[at, :]) * SCALE
            s = jnp.where(keep, s, -1e30)
            e = jnp.exp(s - jnp.max(s, axis=-1, keepdims=True))
            p = (e * (1.0 / jnp.sum(e, axis=-1, keepdims=True))).astype(BF16)
            o = dot_nn(p, jnp.where(here, v_o[:, at], zero))
            for j in range(wide // 128):
                blocks[lo // 128 + j] = blocks[lo // 128 + j] + o[:, j * 128 : (j + 1) * 128]
        att_o[:, pl.ds(base, GROUP_LANES)] = jnp.concatenate(blocks, axis=1).astype(BF16)
        return carry

    lax.fori_loop(0, HEADS // GROUP, group, 0)
    att_t[...] = turn(att_o[...])
    middle = x + (dot_nn(att_o[...], wo[...]) + vec[BO : BO + 1, :])
    mid_o[...] = middle
    n2, _ = norm_stats(middle)
    two = (n2 * vec[GAIN2 : GAIN2 + 1, :] + vec[SHIFT2 : SHIFT2 + 1, :]).astype(BF16)
    two_o[...] = two
    two_t[...] = turn(two)


def up_kernel(rows, nb, steps, core, *refs):
    two, middle, mask, vec, w_up, b_up, w_down = refs[:7]
    cots = refs[7 : 7 + nb]
    act_o, slope_o, gd_o, gd_keep, gd_send = refs[7 + nb : 12 + nb]
    outs = refs[12 + nb : 12 + 2 * nb]
    acc = refs[12 + 2 * nb]
    j = pl.program_id(0)
    c = core[0]

    @pl.when(j == 0)
    def _():
        col = column_of(mask[0:1, :])
        gd = (join(cots, rows).astype(F32) * col).astype(BF16)
        gd_o[...] = gd
        half = gd.shape[1] // 2
        first, second = gd[:, :half], gd[:, half:]
        gd_keep[...] = jnp.where(c == 0, first, second)
        gd_send[...] = jnp.where(c == 0, second, first)

    hidden = dot_nn(two[...], w_up[...]) + b_up[0:1, :]
    cdf = 0.5 * (1.0 + lax.erf(hidden * 0.7071067811865476))
    pdf = jnp.exp(-0.5 * hidden * hidden) * 0.3989422804014327
    act = (hidden * cdf).astype(BF16)
    act_o[...] = turn(act)
    slope_o[...] = cdf + hidden * pdf
    part = dot_nn(act, w_down[...])
    acc[...] = jnp.where(j == 0, part, acc[...] + part)

    @pl.when(j == steps - 1)
    def _():
        col = column_of(mask[0:1, :])
        out = (col * (middle[...] + (acc[...] + vec[BDOWN : BDOWN + 1, :]))).astype(BF16)
        for s in range(nb):
            outs[s][...] = out[s * rows : (s + 1) * rows, :]


def down_send_kernel(core, gd, slope, w_up, w_down, gh_o, bsum, acc):
    j = pl.program_id(0)
    gh = (dot_nt(gd[...], w_down[...]) * slope[...]).astype(BF16)
    gh_o[...] = gh
    bsum[...] = jnp.broadcast_to(colsum(gh), bsum.shape)
    part = dot_nt(gh, w_up[...])
    acc[...] = jnp.where(j == 0, part, acc[...] + part)


def down_keep_kernel(rows, nb, steps, core, *refs):
    gd, slope, w_up, w_down, before, middle, mask, vec = refs[:8]
    cots = refs[8 : 8 + nb]
    gh_o, bsum, gm_o, gb_o, gb_keep, gb_send, sums, acc = refs[8 + nb :]
    j = pl.program_id(0)
    c = core[0]
    gh = (dot_nt(gd[...], w_down[...]) * slope[...]).astype(BF16)
    gh_o[...] = gh
    bsum[...] = jnp.broadcast_to(colsum(gh), bsum.shape)
    acc[...] = jnp.where(j == 0, before[...], acc[...]) + dot_nt(gh, w_up[...])

    @pl.when(j == steps - 1)
    def _():
        grad = acc[...]
        n2, r2 = norm_stats(middle[...])
        col = column_of(mask[0:1, :])
        result = join(cots, rows).astype(F32) * col
        gm = result + norm_back(grad, n2, r2, vec[GAIN2 : GAIN2 + 1, :])
        gm_o[...] = gm
        gb = gm.astype(BF16)
        gb_o[...] = gb
        half = gb.shape[1] // 2
        first, second = gb[:, :half], gb[:, half:]
        gb_keep[...] = jnp.where(c == 0, first, second)
        gb_send[...] = jnp.where(c == 0, second, first)
        sums[0:1, :] = colsum(grad * n2)
        sums[1:2, :] = colsum(grad)
        sums[2:3, :] = colsum(gb)
        sums[3:4, :] = colsum(gd[...])
        sums[4:8, :] = jnp.zeros((4, sums.shape[1]), F32)


def attend_back_kernel(core, gb, q, k, v, mask, wo, keep_o, send_o, gq_o, gk_o, gv_o, sums, ga, qt, kt, vt, gat, gkt, gvt):
    tokens, width = gb.shape
    c = core[0]
    g_att = dot_nt(gb[...], wo[...]).astype(BF16)
    ga[...] = g_att
    gat[...] = turn(g_att)
    qt[...] = turn(q[...])
    kt[...] = turn(k[...])
    vt[...] = turn(v[...])
    keep = mask[0:1, :] > 0.5

    def group(g, carry):
        base = pl.multiple_of(g * GROUP_LANES, 128)
        blocks = [jnp.zeros((tokens, 128), F32) for _ in range(GROUP_LANES // 128)]
        for h, (lo, hi, first, last) in enumerate(windows()):
            wide = hi - lo
            here = head_lanes((tokens, wide), first, last)
            at = pl.ds(base + lo, wide)
            own = pl.ds(pl.multiple_of(base + h * HEAD_DIM, 16), HEAD_DIM)
            zero = jnp.zeros((tokens, wide), BF16)
            s = dot_nn(jnp.where(here, q[:, at], zero), kt[at, :]) * SCALE
            s = jnp.where(keep, s, -1e30)
            e = jnp.exp(s - jnp.max(s, axis=-1, keepdims=True))
            p = e * (1.0 / jnp.sum(e, axis=-1, keepdims=True))
            dp = dot_nn(jnp.where(here, ga[:, at], zero), vt[at, :])
            gvt[own, :] = dot_nn(gat[own, :], p.astype(BF16))
            ds = (p * (dp - jnp.sum(p * dp, axis=-1, keepdims=True))).astype(BF16)
            gkt[own, :] = dot_nn(qt[own, :], ds)
            o = dot_nn(ds, jnp.where(here, k[:, at], zero))
            for j in range(wide // 128):
                blocks[lo // 128 + j] = blocks[lo // 128 + j] + o[:, j * 128 : (j + 1) * 128]
        gq_o[:, pl.ds(base, GROUP_LANES)] = (jnp.concatenate(blocks, axis=1) * SCALE).astype(BF16)
        return carry

    lax.fori_loop(0, HEADS // GROUP, group, 0)
    gq = gq_o[...]
    gk = (jnp.transpose(gkt[...]) * SCALE).astype(BF16)
    gv = jnp.transpose(gvt[...]).astype(BF16)
    gk_o[...] = gk
    gv_o[...] = gv
    sums[0:1, :] = colsum(gq)
    sums[1:2, :] = colsum(gv)
    sums[2:8, :] = jnp.zeros((6, width), F32)
    half = width // 2
    for i, t in enumerate((gq, gk, gv)):
        first, second = t[:, :half], t[:, half:]
        keep_o[:, i * half : (i + 1) * half] = jnp.where(c == 0, first, second)
        send_o[:, i * half : (i + 1) * half] = jnp.where(c == 0, second, first)


def input_back_kernel(rows, nb, *refs):
    slots = refs[:nb]
    gq, gk, gv, wq, wk, wv, gm, vec, down_sums, attend_sums, up_cols = refs[nb : nb + 11]
    outs = refs[nb + 11 : 2 * nb + 11]
    cols_o = refs[2 * nb + 11]
    grad = dot_nt(gq[...], wq[...]) + dot_nt(gk[...], wk[...]) + dot_nt(gv[...], wv[...])
    n1, r1 = norm_stats(join(slots, rows).astype(F32))
    gx = (gm[...] + norm_back(grad, n1, r1, vec[GAIN1 : GAIN1 + 1, :])).astype(BF16)
    for s in range(nb):
        outs[s][...] = gx[s * rows : (s + 1) * rows, :]
    width = gx.shape[1]
    table = jnp.concatenate(
        [
            down_sums[...], attend_sums[...], colsum(grad * n1), colsum(grad),
            jnp.zeros((COLS - 18, width), F32),
        ],
        axis=0,
    )
    cols_o[...] = jnp.transpose(table) + up_cols[...]


def weight_kernel(count, extra, by_rows, cut, place, *refs):
    t = pl.program_id(0)
    parts = []
    for i in range(count):
        left, right, left_got, right_got = refs[4 * i : 4 * i + 4]
        parts.append(dot_nn(left[...], right[...]) + dot_nn(left_got[...], right_got[...]))
    at = 4 * count
    if extra:
        parts.append(refs[at][...])
        at += 1
    a_send, a_keep, b_send, b_keep = refs[at:]
    low = [p.astype(BF16) for p in parts]
    g = low[0] if len(low) == 1 else jnp.concatenate(low, axis=1)
    a, b = (g[:cut, :], g[cut:, :]) if by_rows else (g[:, :cut], g[:, cut:])

    @pl.when(t < 2)
    def _():
        a_send[0] = a

    @pl.when(t >= 2)
    def _():
        a_keep[0] = a

    @pl.when((t == 0) | (t == 3))
    def _():
        b_send[0] = b

    @pl.when((t == 1) | (t == 2))
    def _():
        b_keep[0] = b


def second_kernel(a_keep, a_got, b_keep, b_got, a_o, b_o):
    a_o[...] = (a_keep[0].astype(F32) + a_got[0].astype(F32)).astype(BF16)
    b_o[...] = (b_keep[0].astype(F32) + b_got[0].astype(F32)).astype(BF16)


def third_kernel(nb, size, by_rows, cut, core, band, a_keep, a_got, a_more, b_keep, b_got, b_more, *refs):
    sends, own, held = refs[: 2 * nb - 1], refs[2 * nb - 1], refs[2 * nb]
    a = a_keep[0].astype(F32) + a_got[0].astype(F32) + a_more[...].astype(F32)
    b = b_keep[0].astype(F32) + b_got[0].astype(F32) + b_more[...].astype(F32)
    if by_rows:
        held[:cut, :] = a
        held[cut:, :] = b
    else:
        held[:, :cut] = a
        held[:, cut:] = b
    for i, (t, s) in enumerate(targets(nb)):
        c = core[0] if t == 0 else 1 - core[0]
        block = c * nb + lax.rem(band[0] + s, nb)
        piece = held[pl.ds(pl.multiple_of(block * size, 8), size), :]
        if i == 0:
            own[...] = piece
        else:
            sends[i - 1][...] = piece.astype(BF16)


def last_kernel(nb, widths, extra, core, own, *refs):
    gots, outs = refs[: 2 * nb - 1], refs[2 * nb - 1 :]
    same, other = own[...], None
    for i, (t, _) in enumerate(targets(nb)[1:]):
        got = gots[i][...].astype(F32)
        if t == 0:
            same = same + got
        else:
            other = got if other is None else other + got
    first = core[0] == 0
    at = 0
    for w, out in zip(widths, outs):
        x, y = same[:, at : at + w], other[:, at : at + w]
        out[:, :w] = jnp.where(first, x, y)
        out[:, w:] = jnp.where(first, y, x)
        at += w
    if extra:
        outs[-1][...] = same[:, at:] + other[:, at:]


def targets(nb):
    return [(t, s) for t in range(2) for s in range(nb)]


COLS = 128


VM = pl.BlockSpec(memory_space=pltpu.VMEM)
SM = pl.BlockSpec(memory_space=pltpu.SMEM)


def shape(*dims, dtype=BF16):
    return jax.ShapeDtypeStruct(dims, dtype)


CHEAP = pl.CostEstimate(flops=1000, bytes_accessed=1000, transcendentals=0)


def after(x, *others):
    return lax.optimization_barrier((x, others))[0]


class Links:
    def __init__(self, n_img, n_band):
        self.n_img, self.nb = n_img, n_band
        self.hi = n_img // 8
        i = lax.axis_index("img")
        self.c = i & 1
        self.p = (i >> 1) & 1
        self.q = (i >> 2) & 1
        self.h = i >> 3
        self.b = lax.axis_index("band")

    def flip(self, x, bit):
        return lax.ppermute(x, "img", [(k, k ^ bit) for k in range(self.n_img)])

    def band_shift(self, x, s):
        return lax.ppermute(x, "band", [(k, (k + s) % self.nb) for k in range(self.nb)])

    def hi_shift(self, x, s):
        n = self.n_img
        return lax.ppermute(x, "img", [(k, (k + 8 * s) % n) for k in range(n)])

    def scatter_in(self, x):
        slots = [take(x, self.b, 0)]
        for s in range(1, self.nb):
            blk = take(x, (self.b + s) % self.nb, 0)
            slots.append(self.band_shift(blk, s))
        return slots

    def scatter_back(self, slots):
        got = [slots[0]]
        for s in range(1, self.nb):
            got.append(self.band_shift(slots[s], -s))
        stacked = jnp.stack(got + got)
        return lax.dynamic_slice_in_dim(stacked, (self.nb - self.b) % self.nb, self.nb, axis=0)

    def both_shift(self, x, t, s):
        n, nb = self.n_img, self.nb
        perm = [(k * nb + b, (k ^ t) * nb + (b + s) % nb) for k in range(n) for b in range(nb)]
        return lax.ppermute(x, ("img", "band"), perm)


class Unit:
    def __init__(self, links, pairs, extra=None, by_rows=False):
        self.links, self.by_rows, self.extra = links, by_rows, extra is not None
        hi = links.hi
        total_rows, tokens = pairs[0][0].shape
        self.block = total_rows // 4
        self.widths = [p[1].shape[1] for p in pairs]
        self.cols = sum(self.widths) + (extra.shape[1] if self.extra else 0)
        block, cols = self.block, self.cols
        self.cut = block // 2 if by_rows else -(-cols // 256) * 128

        def order(x):
            if hi == 1:
                return x
            return x.reshape(hi, 4, -1, x.shape[1]).swapaxes(0, 1).reshape(x.shape)

        which = lambda t, pq: ((pq[1] ^ ((t == 0) | (t == 3)).astype(jnp.int32)) * 2 + (pq[0] ^ (t < 2).astype(jnp.int32)), 0)
        args, specs = [], []
        for left, right, left_got, right_got in pairs:
            args += [order(left), right, order(left_got), right_got]
            l_spec = pl.BlockSpec((block, tokens), which)
            r_spec = pl.BlockSpec((tokens, right.shape[1]), lambda t, pq: (0, 0))
            specs += [l_spec, r_spec, l_spec, r_spec]
        if self.extra:
            args.append(order(extra))
            specs.append(pl.BlockSpec((block, extra.shape[1]), which))
        a_dims = (self.cut, cols) if by_rows else (block, self.cut)
        b_dims = (block - self.cut, cols) if by_rows else (block, cols - self.cut)
        self.dims = (a_dims, b_dims)
        out = lambda dims, f: pl.BlockSpec((1,) + dims, lambda t, pq: (f(t), 0, 0))
        one = lambda c: c.astype(jnp.int32)
        pq = jnp.stack([links.p, links.q]).astype(jnp.int32)
        self.a_send, self.a_keep, self.b_send, self.b_keep = pl.pallas_call(
            functools.partial(weight_kernel, len(pairs), self.extra, by_rows, self.cut),
            grid_spec=pltpu.PrefetchScalarGridSpec(
                num_scalar_prefetch=1,
                grid=(4,),
                in_specs=specs,
                out_specs=[
                    out(a_dims, lambda t: one(t == 0)),
                    out(a_dims, lambda t: one(t == 3)),
                    out(b_dims, lambda t: one(t == 0)),
                    out(b_dims, lambda t: one(t < 2)),
                ],
            ),
            out_shape=[shape(2, *a_dims)] * 2 + [shape(2, *b_dims)] * 2,
            cost_estimate=CHEAP,
            name="weight_grad",
        )(pq, *args)

    def start(self):
        self.a_got = self.links.flip(self.a_send, 2)
        self.b_got = self.links.flip(self.b_send, 4)

    def second(self, *deps):
        a_dims, b_dims = self.dims
        pick = lambda dims: pl.BlockSpec((1,) + dims, lambda i: (1, 0, 0))
        whole = lambda dims: pl.BlockSpec(dims, lambda i: (0, 0))
        a, b = pl.pallas_call(
            second_kernel,
            grid=(1,),
            in_specs=[pick(a_dims)] * 2 + [pick(b_dims)] * 2,
            out_specs=[whole(a_dims), whole(b_dims)],
            out_shape=[shape(*a_dims), shape(*b_dims)],
            cost_estimate=CHEAP,
            name="second",
        )(after(self.a_keep, *deps), self.a_got, self.b_keep, self.b_got)
        self.a_more = self.links.flip(a, 4)
        self.b_more = self.links.flip(b, 2)
        return a

    def third(self, *deps):
        links, nb = self.links, self.links.nb
        size = self.block // (links.hi * 2 * nb)
        self.size = size
        a_dims, b_dims = self.dims
        a_keep = after(self.a_keep, *deps)
        if links.hi > 1 or size % 8:
            a = a_keep[0].astype(F32) + self.a_got[0].astype(F32) + self.a_more.astype(F32)
            b = self.b_keep[0].astype(F32) + self.b_got[0].astype(F32) + self.b_more.astype(F32)
            held = jnp.concatenate([a, b], axis=0 if self.by_rows else 1)
            held = held.reshape(links.hi, 2 * nb * size, self.cols)
            total = take(held, links.h, 0)
            for s in range(1, links.hi):
                total = total + links.hi_shift(take(held, (links.h + s) % links.hi, 0).astype(BF16), s).astype(F32)
            held = total.reshape(2, nb, size, self.cols)
            pieces = [take(take(held, links.c ^ t, 0), (links.b + s) % nb, 0) for t, s in targets(nb)]
            self.own, sends = pieces[0], [x.astype(BF16) for x in pieces[1:]]
        else:
            pick = lambda dims: pl.BlockSpec((1,) + dims, lambda i: (0, 0, 0))
            whole = lambda dims: pl.BlockSpec(dims, lambda i: (0, 0))
            scalar = lambda x: x.astype(jnp.int32).reshape(1)
            *sends, self.own = pl.pallas_call(
                functools.partial(third_kernel, nb, size, self.by_rows, self.cut),
                grid=(1,),
                in_specs=[SM, SM] + [pick(a_dims)] * 2 + [whole(a_dims)] + [pick(b_dims)] * 2 + [whole(b_dims)],
                out_specs=[whole((size, self.cols))] * (2 * nb),
                out_shape=[shape(size, self.cols)] * (2 * nb - 1) + [shape(size, self.cols, dtype=F32)],
                scratch_shapes=[pltpu.VMEM((self.block, self.cols), F32)],
                cost_estimate=CHEAP,
                name="third",
            )(
                scalar(links.c), scalar(links.b), a_keep, self.a_got, self.a_more,
                self.b_keep, self.b_got, self.b_more,
            )
        self.gots = [links.both_shift(x, t, s) for x, (t, s) in zip(sends, targets(nb)[1:])]
        return self.own

    def last(self, *deps):
        links, nb, size = self.links, self.links.nb, self.size
        outs = [shape(size, 2 * w, dtype=F32) for w in self.widths]
        if self.extra:
            outs.append(shape(size, COLS, dtype=F32))
        return pl.pallas_call(
            functools.partial(last_kernel, nb, self.widths, self.extra),
            in_specs=[SM] + [VM] * (2 * nb),
            out_specs=[VM] * len(outs),
            out_shape=outs,
            cost_estimate=CHEAP,
            name="last",
        )(links.c.astype(jnp.int32).reshape(1), after(self.own, *deps), *self.gots)


def per_device(
    inputs, keep_mask, crop_rows, crop_cols, gain_one, shift_one, w_query, b_query, w_key, w_value,
    b_value, w_out, b_out, gain_two, shift_two, w_up, b_up, w_down, b_down, cotangent, *, n_img, nb,
):
    images, rows, width = inputs.shape
    hidden_width = w_up.shape[1]
    assert images == nb
    tokens = nb * rows
    links = Links(n_img, nb)
    core = links.c.astype(jnp.int32).reshape(1)
    f = lambda v: v.astype(F32)
    position = links.b * rows + jnp.arange(rows, dtype=jnp.int32)
    inside = (
        (keep_mask > 0)
        & (position[None, :] // SIDE < crop_rows[:, None])
        & (position[None, :] % SIDE < crop_cols[:, None])
    )
    flags = jnp.tile(inside.astype(BF16), (1, nb))[:, None, :]
    slot_of = jnp.arange(tokens, dtype=jnp.int32) // rows
    flags = jnp.where(jnp.arange(8)[None, :, None] == slot_of[None, None, :], flags, jnp.zeros((), BF16))
    flags = jnp.pad(flags, ((0, 0), (0, 0), (0, width - tokens)))
    packed = jnp.concatenate([inputs, flags], axis=1)
    slots = links.scatter_in(packed)
    later = lax.optimization_barrier((cotangent, slots[nb - 1], slots[1], slots[2 % nb]))
    cots = links.scatter_in(later[0])
    vec = jnp.stack([f(t) for t in (gain_one, shift_one, b_query, b_value, b_out, gain_two, shift_two, b_down)])
    b_up_row = f(b_up)[None, :]

    full = shape(tokens, width)
    tall_t = shape(width, tokens)
    normed_t, q, k, v, attended_t, middle, two, two_t, mask = pl.pallas_call(
        functools.partial(attend_kernel, rows, nb),
        in_specs=[VM] * (nb + 5),
        out_specs=[VM] * 9,
        out_shape=[tall_t] + [full] * 3 + [tall_t, shape(tokens, width, dtype=F32), full, tall_t, shape(8, tokens, dtype=F32)],
        scratch_shapes=[pltpu.VMEM((tokens, width), BF16), pltpu.VMEM((width, tokens), BF16)],
        cost_estimate=CHEAP,
        name="attend",
    )(*slots, vec, w_query, w_key, w_value, w_out)

    attended_got = links.flip(attended_t, 1)
    normed_got = links.flip(normed_t, 1)
    two_got = links.flip(two_t, 1)

    steps = 4
    block = hidden_width // steps
    half = width // 2
    fixed = lambda *dims: pl.BlockSpec(dims, lambda j, c: (0,) * len(dims))
    tall = lambda *dims: pl.BlockSpec(dims, lambda j, c: (0, j))
    up = pl.pallas_call(
        functools.partial(up_kernel, rows, nb, steps),
        grid_spec=pltpu.PrefetchScalarGridSpec(
            num_scalar_prefetch=1,
            grid=(steps,),
            in_specs=[
                fixed(tokens, width), fixed(tokens, width), fixed(8, tokens), fixed(8, width),
                tall(width, block), tall(1, block),
                pl.BlockSpec((block, width), lambda j, c: (j, 0)),
            ] + [fixed(rows, width)] * nb,
            out_specs=[
                pl.BlockSpec((block, tokens), lambda j, c: (j, 0)), tall(tokens, block), fixed(tokens, width),
                fixed(tokens, half), fixed(tokens, half),
            ] + [fixed(rows, width)] * nb,
            scratch_shapes=[pltpu.VMEM((tokens, width), F32)],
        ),
        out_shape=[
            shape(hidden_width, tokens), shape(tokens, hidden_width, dtype=F32), full,
            shape(tokens, half), shape(tokens, half),
        ] + [shape(rows, width)] * nb,
        cost_estimate=CHEAP,
        name="up",
    )(core, two, middle, mask, vec, w_up, b_up_row, w_down, *cots)
    activated_t, slope, grad_down, gd_keep, gd_send = up[:5]
    out_slots = up[5:]
    act_got = links.flip(activated_t, 1)
    gd_got = links.flip(gd_send, 1)
    output = links.scatter_back(out_slots)

    def halves(sending):
        offset = lambda c: 2 * (1 - c[0]) if sending else 2 * c[0]
        wide = lambda *dims: pl.BlockSpec(dims, lambda j, c: (0, j + offset(c)))
        return [
            fixed(tokens, width), wide(tokens, block), wide(width, block),
            pl.BlockSpec((block, width), lambda j, c: (j + offset(c), 0)),
        ]

    gh_send, send_sum, before = pl.pallas_call(
        down_send_kernel,
        grid_spec=pltpu.PrefetchScalarGridSpec(
            num_scalar_prefetch=1,
            grid=(steps // 2,),
            in_specs=halves(True),
            out_specs=[tall(tokens, block), tall(8, block), fixed(tokens, width)],
        ),
        out_shape=[
            shape(tokens, hidden_width // 2), shape(8, hidden_width // 2, dtype=F32),
            shape(tokens, width, dtype=F32),
        ],
        cost_estimate=CHEAP,
        name="down_send",
    )(core, grad_down, slope, w_up, w_down)
    gh_got = links.flip(gh_send, 1)

    unit_down = Unit(links, [(after(activated_t, before), gd_keep, act_got, gd_got)], by_rows=True)
    unit_down.start()

    gh_keep, keep_sum, grad_middle, grad_branch, gb_keep, gb_send, down_sums = pl.pallas_call(
        functools.partial(down_keep_kernel, rows, nb, steps // 2),
        grid_spec=pltpu.PrefetchScalarGridSpec(
            num_scalar_prefetch=1,
            grid=(steps // 2,),
            in_specs=halves(False)
            + [fixed(tokens, width), fixed(tokens, width), fixed(8, tokens), fixed(8, width)]
            + [fixed(rows, width)] * nb,
            out_specs=[
                tall(tokens, block), tall(8, block), fixed(tokens, width), fixed(tokens, width),
                fixed(tokens, half), fixed(tokens, half), fixed(8, width),
            ],
            scratch_shapes=[pltpu.VMEM((tokens, width), F32)],
        ),
        out_shape=[
            shape(tokens, hidden_width // 2), shape(8, hidden_width // 2, dtype=F32),
            shape(tokens, width, dtype=F32), full, shape(tokens, half), shape(tokens, half),
            shape(8, width, dtype=F32),
        ],
        cost_estimate=CHEAP,
        name="down_keep",
    )(core, after(grad_down, unit_down.a_send), slope, w_up, w_down, before, middle, mask, vec, *cots)
    gb_got = links.flip(gb_send, 1)

    unit_up = Unit(
        links, [(two_t, gh_keep, two_got, gh_got), (attended_t, gb_keep, attended_got, gb_got)]
    )
    unit_up.start()

    low = lambda: pltpu.VMEM((width, tokens), BF16)
    qkv_keep, qkv_send, gq, gk, gv, attend_sums = pl.pallas_call(
        attend_back_kernel,
        in_specs=[SM] + [VM] * 6,
        out_specs=[VM] * 6,
        out_shape=[shape(tokens, 3 * half)] * 2 + [full] * 3 + [shape(8, width, dtype=F32)],
        scratch_shapes=[
            pltpu.VMEM((tokens, width), BF16), low(), low(), low(), low(),
            pltpu.VMEM((width, tokens), F32), pltpu.VMEM((width, tokens), F32),
        ],
        cost_estimate=CHEAP,
        name="attend_back",
    )(core, after(grad_branch, unit_up.a_send), q, k, v, mask, w_out)
    qkv_got = links.flip(qkv_send, 1)

    mark = unit_down.second(attend_sums)

    first = jnp.where(links.c == 0, keep_sum[0], send_sum[0])
    other = jnp.where(links.c == 0, send_sum[0], keep_sum[0])
    up_cols = jnp.concatenate([first, other]).reshape(width, hidden_width // width)
    up_cols = jnp.pad(up_cols, ((0, 0), (18, COLS - 18 - hidden_width // width)))
    back = pl.pallas_call(
        functools.partial(input_back_kernel, rows, nb),
        in_specs=[VM] * (nb + 11),
        out_specs=[VM] * (nb + 1),
        out_shape=[shape(rows, width)] * nb + [shape(width, COLS, dtype=F32)],
        cost_estimate=CHEAP,
        name="input_back",
    )(
        *slots, after(gq, mark), gk, gv, w_query, w_key, w_value, grad_middle, vec, down_sums, attend_sums, up_cols,
    )
    unit_qkv = Unit(links, [(normed_t, qkv_keep, normed_got, qkv_got)], extra=back[nb])
    unit_qkv.widths = [half] * 3
    unit_qkv.start()
    grad_inputs = links.scatter_back(back[:nb])

    mark = unit_up.second(unit_qkv.a_send)
    mark = unit_down.third(mark)
    output = after(output, mark)
    mark = unit_qkv.second(mark)
    mark = unit_up.third(mark)
    (g_w_down,) = unit_down.last(mark)
    mark = unit_qkv.third(g_w_down)
    g_w_up, g_w_out = unit_up.last(mark)
    g_w_query, g_w_key, g_w_value, cols = unit_qkv.last(g_w_up)
    sums = [cols[:, i] for i in range(18)]
    g_b_up = cols[:, 18 : 18 + hidden_width // width].reshape(-1)
    return (
        output.reshape(inputs.shape),
        grad_inputs.astype(F32).reshape(inputs.shape),
        sums[16],
        sums[17],
        g_w_query,
        sums[8],
        g_w_key,
        g_w_value,
        sums[9],
        g_w_out,
        sums[2],
        sums[0],
        sums[1],
        g_w_up,
        g_b_up,
        g_w_down,
        sums[3],
    )


def solution(mesh):
    n_img, nb = mesh.shape["img"], mesh.shape["band"]

    def body(*args):
        return per_device(*args, n_img=n_img, nb=nb)

    both = P(("img", "band"))
    rows = P(("img", "band"), None)
    token = P("img", "band", None)
    return jax.shard_map(
        body,
        mesh=mesh,
        in_specs=(token, P("img", "band"), P("img"), P("img")) + (P(),) * 15 + (token,),
        out_specs=(
            token, token, both, both, rows, both, rows, rows, both, rows, both, both, both, rows, both,
            rows, both,
        ),
        check_vma=False,
    )
```

```python
import functools

import jax
import jax.numpy as jnp
from jax import lax
from jax.experimental import pallas as pl
from jax.experimental.pallas import tpu as pltpu
from jax.sharding import PartitionSpec as P

HEADS = 16
HEAD_DIM = 48
SIDE = 16
EPS = 1e-05
F32 = jnp.float32
BF16 = jnp.bfloat16
GROUP = 8
GROUP_LANES = GROUP * HEAD_DIM
SCALE = HEAD_DIM ** (-0.5)


def dot_nn(a, b):
    return lax.dot_general(a, b, (((1,), (0,)), ((), ())), preferred_element_type=F32)


def dot_nt(a, b):
    return lax.dot_general(a, b, (((1,), (1,)), ((), ())), preferred_element_type=F32)


def dot_tn(a, b):
    return lax.dot_general(a, b, (((0,), (0,)), ((), ())), preferred_element_type=F32)


def norm_stats(x):
    mean = jnp.mean(x, axis=-1, keepdims=True)
    centred = x - mean
    var = jnp.mean(centred * centred, axis=-1, keepdims=True)
    r = lax.rsqrt(var + EPS)
    return centred * r, r


def norm_back(grad, n, r, gain):
    e = grad * gain
    return r * (e - jnp.mean(e, axis=-1, keepdims=True) - n * jnp.mean(e * n, axis=-1, keepdims=True))


def colsum(x):
    return jnp.sum(x.astype(F32), axis=0, keepdims=True)


def take(x, index, axis):
    return lax.dynamic_index_in_dim(x, index, axis, keepdims=False)


GAIN1, SHIFT1, BQ, BV, BO, GAIN2, SHIFT2, BDOWN = range(8)


def windows():
    out = []
    for h in range(GROUP):
        first, last = h * HEAD_DIM, (h + 1) * HEAD_DIM
        lo, hi = first // 128 * 128, -(-last // 128) * 128
        out.append((lo, hi, first - lo, last - lo))
    return out


def head_lanes(shape, first, last):
    lane = lax.broadcasted_iota(jnp.int32, shape, 1)
    return (lane >= first) & (lane < last)


def turn(x):
    return jnp.transpose(x.astype(F32)).astype(BF16)


def split_rows(x, block, c, keep, send, at=0):
    for i in range(x.shape[0] // (2 * block)):
        even, odd = x[2 * i * block : (2 * i + 1) * block, :], x[(2 * i + 1) * block : (2 * i + 2) * block, :]
        rows = pl.ds(at + i * block, block)
        keep[rows, :] = jnp.where(c == 0, even, odd)
        send[rows, :] = jnp.where(c == 0, odd, even)


def join(refs, rows):
    return jnp.concatenate([r[:rows, :] for r in refs], axis=0)


def column_of(row):
    n = row.shape[1]
    eye = lax.broadcasted_iota(jnp.int32, (n, n), 0) == lax.broadcasted_iota(jnp.int32, (n, n), 1)
    return jnp.sum(jnp.where(eye, row, 0.0), axis=1, keepdims=True)


def attend_kernel(rows, nb, block, core, *refs):
    slots = refs[:nb]
    c = core[0]
    vec, wq, wk, wv, wo = refs[nb : nb + 5]
    keep_o, send_o, q_o, k_o, v_o, mid_o, two_o, mask_o, att_o, kt = refs[nb + 5 :]
    tokens = nb * rows
    half = q_o.shape[1] // 2
    row = jnp.zeros((1, tokens), F32)
    for s in range(nb):
        row = row + slots[s][rows : rows + 8, :tokens].astype(F32)[s : s + 1, :]
    mask_o[...] = jnp.broadcast_to(row, mask_o.shape)
    x = join(slots, rows).astype(F32)
    n1, _ = norm_stats(x)
    normed = (n1 * vec[GAIN1 : GAIN1 + 1, :] + vec[SHIFT1 : SHIFT1 + 1, :]).astype(BF16)
    split_rows(turn(normed), block, c, keep_o, send_o)
    q_o[...] = (dot_nn(normed, wq[...]) + vec[BQ : BQ + 1, :]).astype(BF16)
    k = dot_nn(normed, wk[...]).astype(BF16)
    k_o[...] = k
    kt[...] = turn(k)
    v_o[...] = (dot_nn(normed, wv[...]) + vec[BV : BV + 1, :]).astype(BF16)
    keep = row > 0.5

    def group(g, carry):
        base = pl.multiple_of(g * GROUP_LANES, 128)
        blocks = [jnp.zeros((tokens, 128), F32) for _ in range(GROUP_LANES // 128)]
        for lo, hi, first, last in windows():
            wide = hi - lo
            here = head_lanes((tokens, wide), first, last)
            at = pl.ds(base + lo, wide)
            zero = jnp.zeros((tokens, wide), BF16)
            qm = jnp.where(here, q_o[:, at], zero)
            s = dot_nn(qm, kt[at, :]) * SCALE
            s = jnp.where(keep, s, -1e30)
            e = jnp.exp(s - jnp.max(s, axis=-1, keepdims=True))
            p = (e * (1.0 / jnp.sum(e, axis=-1, keepdims=True))).astype(BF16)
            o = dot_nn(p, jnp.where(here, v_o[:, at], zero))
            for j in range(wide // 128):
                blocks[lo // 128 + j] = blocks[lo // 128 + j] + o[:, j * 128 : (j + 1) * 128]
        att_o[:, pl.ds(base, GROUP_LANES)] = jnp.concatenate(blocks, axis=1).astype(BF16)
        return carry

    lax.fori_loop(0, HEADS // GROUP, group, 0)
    split_rows(turn(att_o[...]), block, c, keep_o, send_o, half)
    middle = x + (dot_nn(att_o[...], wo[...]) + vec[BO : BO + 1, :])
    mid_o[...] = middle
    n2, _ = norm_stats(middle)
    two = (n2 * vec[GAIN2 : GAIN2 + 1, :] + vec[SHIFT2 : SHIFT2 + 1, :]).astype(BF16)
    two_o[...] = two
    split_rows(turn(two), block, c, keep_o, send_o, 2 * half)


def up_kernel(rows, nb, steps, block, core, *refs):
    two, middle, mask, vec, w_up, b_up, w_down = refs[:7]
    cots = refs[7 : 7 + nb]
    act_keep, act_send, right_o, bsum = refs[7 + nb : 11 + nb]
    outs = refs[11 + nb : 11 + 2 * nb]
    acc = refs[11 + 2 * nb]
    j = pl.program_id(0)
    width = acc.shape[1]

    @pl.when(j == 0)
    def _():
        col = column_of(mask[0:1, :])
        right_o[:, :width] = (join(cots, rows).astype(F32) * col).astype(BF16)

    hidden = dot_nn(two[...], w_up[...]) + b_up[0:1, :]
    cdf = 0.5 * (1.0 + lax.erf(hidden * 0.7071067811865476))
    pdf = jnp.exp(-0.5 * hidden * hidden) * 0.3989422804014327
    act = (hidden * cdf).astype(BF16)
    split_rows(turn(act), block, core[0], act_keep, act_send)
    part = dot_nn(act, w_down[...])
    acc[...] = jnp.where(j == 0, part, acc[...] + part)
    gh = (dot_nt(right_o[:, :width], w_down[...]) * (cdf + hidden * pdf)).astype(BF16)
    right_o[:, pl.ds(pl.multiple_of(width + j * gh.shape[1], 128), gh.shape[1])] = gh
    bsum[...] = jnp.broadcast_to(colsum(gh), bsum.shape)

    @pl.when(j == steps - 1)
    def _():
        col = column_of(mask[0:1, :])
        out = (col * (middle[...] + (acc[...] + vec[BDOWN : BDOWN + 1, :]))).astype(BF16)
        for s in range(nb):
            outs[s][...] = out[s * rows : (s + 1) * rows, :]


def down_kernel(rows, nb, steps, *refs):
    gd, gh, w_up, middle, mask, vec = refs[:6]
    cots = refs[6 : 6 + nb]
    gm_o, gb_o, sums, acc = refs[6 + nb :]
    j = pl.program_id(0)
    part = dot_nt(gh[...], w_up[...])
    acc[...] = jnp.where(j == 0, part, acc[...] + part)

    @pl.when(j == steps - 1)
    def _():
        grad = acc[...]
        n2, r2 = norm_stats(middle[...])
        col = column_of(mask[0:1, :])
        result = join(cots, rows).astype(F32) * col
        gm = result + norm_back(grad, n2, r2, vec[GAIN2 : GAIN2 + 1, :])
        gm_o[...] = gm
        gb = gm.astype(BF16)
        gb_o[...] = gb
        sums[0:1, :] = colsum(grad * n2)
        sums[1:2, :] = colsum(grad)
        sums[2:3, :] = colsum(gb)
        sums[3:4, :] = colsum(gd[...])
        sums[4:8, :] = jnp.zeros((4, sums.shape[1]), F32)


def attend_back_kernel(gb, q, k, v, mask, wo, right_o, sums, gq_o, ga, qt, kt, vt, gat, gkt, gvt):
    tokens, width = gb.shape
    g_att = dot_nt(gb[...], wo[...]).astype(BF16)
    ga[...] = g_att
    gat[...] = turn(g_att)
    qt[...] = turn(q[...])
    kt[...] = turn(k[...])
    vt[...] = turn(v[...])
    keep = mask[0:1, :] > 0.5

    def group(g, carry):
        base = pl.multiple_of(g * GROUP_LANES, 128)
        blocks = [jnp.zeros((tokens, 128), F32) for _ in range(GROUP_LANES // 128)]
        for h, (lo, hi, first, last) in enumerate(windows()):
            wide = hi - lo
            here = head_lanes((tokens, wide), first, last)
            at = pl.ds(base + lo, wide)
            own = pl.ds(pl.multiple_of(base + h * HEAD_DIM, 16), HEAD_DIM)
            zero = jnp.zeros((tokens, wide), BF16)
            s = dot_nn(jnp.where(here, q[:, at], zero), kt[at, :]) * SCALE
            s = jnp.where(keep, s, -1e30)
            e = jnp.exp(s - jnp.max(s, axis=-1, keepdims=True))
            p = e * (1.0 / jnp.sum(e, axis=-1, keepdims=True))
            dp = dot_nn(jnp.where(here, ga[:, at], zero), vt[at, :])
            gvt[own, :] = dot_nn(gat[own, :], p.astype(BF16))
            ds = (p * (dp - jnp.sum(p * dp, axis=-1, keepdims=True))).astype(BF16)
            gkt[own, :] = dot_nn(qt[own, :], ds)
            o = dot_nn(ds, jnp.where(here, k[:, at], zero))
            for j in range(wide // 128):
                blocks[lo // 128 + j] = blocks[lo // 128 + j] + o[:, j * 128 : (j + 1) * 128]
        gq_o[:, pl.ds(base, GROUP_LANES)] = (jnp.concatenate(blocks, axis=1) * SCALE).astype(BF16)
        return carry

    lax.fori_loop(0, HEADS // GROUP, group, 0)
    gq = gq_o[...]
    gk = (jnp.transpose(gkt[...]) * SCALE).astype(BF16)
    gv = jnp.transpose(gvt[...]).astype(BF16)
    for i, t in enumerate((gq, gk, gv)):
        right_o[:, i * width : (i + 1) * width] = t
    sums[0:1, :] = colsum(gq)
    sums[1:2, :] = colsum(gv)
    sums[2:8, :] = jnp.zeros((6, width), F32)


def input_back_kernel(rows, nb, block, core, *refs):
    slots = refs[:nb]
    right, wq, wk, wv, gm, vec, down_sums, attend_sums = refs[nb : nb + 8]
    outs = refs[nb + 8 : 2 * nb + 8]
    keep_o, send_o = refs[2 * nb + 8 :]
    width = gm.shape[1]
    grad = dot_nt(right[:, :width], wq[...])
    grad = grad + dot_nt(right[:, width : 2 * width], wk[...])
    grad = grad + dot_nt(right[:, 2 * width :], wv[...])
    n1, r1 = norm_stats(join(slots, rows).astype(F32))
    gx = (gm[...] + norm_back(grad, n1, r1, vec[GAIN1 : GAIN1 + 1, :])).astype(BF16)
    for s in range(nb):
        outs[s][...] = gx[s * rows : (s + 1) * rows, :]
    table = jnp.concatenate(
        [
            down_sums[...], attend_sums[...], colsum(grad * n1), colsum(grad),
            jnp.zeros((COLS - 18, width), F32),
        ],
        axis=0,
    )
    split_rows(jnp.transpose(table), block, core[0], keep_o, send_o)


def spread_kernel(rows, nb, band, crop_rows, crop_cols, x, keep_mask, *outs):
    width = x.shape[2]
    position = band[0] * rows + lax.broadcasted_iota(jnp.int32, (1, rows), 1)
    slot = lax.broadcasted_iota(jnp.int32, (8, width), 0)
    lane = lax.broadcasted_iota(jnp.int32, (8, width), 1) // rows
    for s in range(nb):
        image = lax.rem(band[0] + s, nb)
        outs[s][:rows, :] = x[image]
        inside = (
            (keep_mask[pl.ds(image, 1), :] > 0)
            & (position // SIDE < crop_rows[image])
            & (position % SIDE < crop_cols[image])
        )
        flags = jnp.concatenate([jnp.where(inside, 1.0, 0.0)] * (width // rows), axis=1)
        outs[s][rows:, :] = jnp.where((slot == s) & (lane == s), flags, 0.0).astype(BF16)


def gather_kernel(nb, band, *refs):
    for s in range(nb):
        image = lax.rem(band[0] + s, nb)
        refs[2 * nb][image] = refs[s][...]
        refs[2 * nb + 1][image] = refs[nb + s][...].astype(F32)


def weight_kernel(groups, quarters, *refs):
    t = pl.program_id(0)
    parts, at = [], 0
    for widths in groups:
        left, left_got = refs[at : at + 2]
        at += 2
        for _ in widths:
            right, right_got = refs[at : at + 2]
            at += 2
            parts.append((dot_nn(left[...], right[...]) + dot_nn(left_got[...], right_got[...])).astype(BF16))
    send, keep = refs[at:]
    g = parts[0] if len(parts) == 1 else jnp.concatenate(parts, axis=1)

    @pl.when(t < 2)
    def _():
        send[0] = g

    @pl.when(t >= 2)
    def _():
        keep[0] = g


def second_kernel(keep, got, out):
    out[...] = (keep[0].astype(F32) + got[0].astype(F32)).astype(BF16)


def third_kernel(size, band, keep, got, more, keep_o, send_o, held):
    held[...] = keep[0].astype(F32) + got[0].astype(F32) + more[...].astype(F32)
    for i in range(2):
        near = jnp.bitwise_xor(band[0], 2 * i)
        far = jnp.bitwise_xor(band[0], 2 * i + 1)
        keep_o[i] = held[pl.ds(pl.multiple_of(near * size, 8), size), :]
        send_o[i] = held[pl.ds(pl.multiple_of(far * size, 8), size), :].astype(BF16)


def last_kernel(widths, keep, got, more, *outs):
    at = 0
    for w, out in zip(widths, outs):
        cols = pl.ds(at, w)
        out[...] = keep[0, :, cols] + got[0, :, cols].astype(F32) + more[:, cols].astype(F32)
        at += w


COLS = 128


VM = pl.BlockSpec(memory_space=pltpu.VMEM)
SM = pl.BlockSpec(memory_space=pltpu.SMEM)


def shape(*dims, dtype=BF16):
    return jax.ShapeDtypeStruct(dims, dtype)


def cost(us):
    return pl.CostEstimate(flops=us * 2500000000, bytes_accessed=us * 10000000, transcendentals=0)


def after(x, *others):
    return lax.optimization_barrier((x, others))[0]


def scalar(x):
    return x.astype(jnp.int32).reshape(1)


class Links:
    def __init__(self, n_img, n_band):
        self.n_img, self.nb = n_img, n_band
        self.hi = n_img // 8
        i = lax.axis_index("img")
        self.c = i & 1
        self.p = (i >> 1) & 1
        self.q = (i >> 2) & 1
        self.h = i >> 3
        self.b = lax.axis_index("band")

    def flip(self, x, bit):
        return lax.ppermute(x, "img", [(k, k ^ bit) for k in range(self.n_img)])

    def flip_by_core(self, x, even, odd):
        return lax.ppermute(x, "img", [(k, k ^ (odd if k & 1 else even)) for k in range(self.n_img)])

    def flip_band(self, x, bit):
        return lax.ppermute(x, "band", [(k, k ^ bit) for k in range(self.nb)])

    def band_shift(self, x, s):
        return lax.ppermute(x, "band", [(k, (k + s) % self.nb) for k in range(self.nb)])

    def hi_shift(self, x, s):
        n = self.n_img
        return lax.ppermute(x, "img", [(k, (k + 8 * s) % n) for k in range(n)])

    def sum_hi(self, x):
        x = x.reshape(self.hi, x.shape[0] // self.hi, *x.shape[1:])
        total = take(x, self.h, 0)
        for s in range(1, self.hi):
            total = total + self.hi_shift(take(x, (self.h + s) % self.hi, 0).astype(BF16), s).astype(F32)
        return total

    def by_quarter(self, x):
        if self.hi == 1:
            return x
        return x.reshape(self.hi, 4, -1, x.shape[1]).swapaxes(0, 1).reshape(x.shape)

    def reclass(self, first, second, block):
        x = jnp.concatenate([first, second], axis=0)
        x = x.reshape(-1, 2, block, x.shape[1])
        own, other = take(x, self.c, 1), take(x, 1 - self.c, 1)
        return own.reshape(-1, x.shape[3]), other.reshape(-1, x.shape[3])


class Unit:
    def __init__(self, links, rows, groups):
        self.links = links
        args, specs, widths = [], [], []
        tokens = groups[0][0].shape[1]
        self.block = block = rows // 4
        for left, left_got, left_at, rights in groups:
            if links.hi > 1:
                left, left_got = (x[left_at * rows : (left_at + 1) * rows, :] for x in (left, left_got))
                left_at = 0
            args += [links.by_quarter(left), links.by_quarter(left_got)]
            specs += [pl.BlockSpec((block, tokens), lambda t, s, i=4 * left_at: (s[t] + i, 0))] * 2
            widths.append([w for w, _, _, _, _ in rights])
            for w, own, own_at, got, got_at in rights:
                args += [own, got]
                specs.append(pl.BlockSpec((tokens, w), lambda t, s, i=own_at: (0, i)))
                specs.append(pl.BlockSpec((tokens, w), lambda t, s, i=got_at: (0, i)))
        self.widths = [w for ws in widths for w in ws]
        self.cols = cols = sum(self.widths)
        p, q = links.p, links.q
        even = links.c == 0
        at = lambda a, b: a * 2 + b
        quarters = jnp.stack(
            [
                jnp.where(even, at(q, 1 - p), at(1 - q, p)), at(1 - q, 1 - p),
                jnp.where(even, at(1 - q, p), at(q, 1 - p)), at(q, p),
            ]
        ).astype(jnp.int32)
        one = lambda x: jnp.asarray(x).astype(jnp.int32)
        self.send, self.keep = pl.pallas_call(
            functools.partial(weight_kernel, widths),
            grid_spec=pltpu.PrefetchScalarGridSpec(
                num_scalar_prefetch=1,
                grid=(4,),
                in_specs=specs,
                out_specs=[
                    pl.BlockSpec((1, block, cols), lambda t, s: (one(t > 0), 0, 0)),
                    pl.BlockSpec((1, block, cols), lambda t, s: (one(t < 3), 0, 0)),
                ],
            ),
            out_shape=[shape(2, block, cols)] * 2,
            cost_estimate=cost(6),
            name="weight_grad",
        )(quarters, *args)
        self.got = links.flip_by_core(self.send, 2, 4)

    def pick(self, i):
        return pl.BlockSpec((1, self.block, self.cols), lambda _: (i, 0, 0))

    def whole(self, *dims):
        return pl.BlockSpec(dims, lambda _: (0,) * len(dims))

    def second(self, *deps):
        dims = (self.block, self.cols)
        sent = pl.pallas_call(
            second_kernel,
            grid=(1,),
            in_specs=[self.pick(1)] * 2,
            out_specs=self.whole(*dims),
            out_shape=shape(*dims),
            cost_estimate=cost(2),
            name="second",
        )(after(self.keep, *deps), self.got)
        self.more = self.links.flip_by_core(sent, 4, 2)
        return sent

    def third(self, *deps):
        links, nb, cols = self.links, self.links.nb, self.cols
        self.size = size = self.block // (links.hi * nb)
        keep = after(self.keep, *deps)
        if links.hi > 1 or size % 8:
            held = links.sum_hi(keep[0].astype(F32) + self.got[0].astype(F32) + self.more.astype(F32))
            held = held.reshape(nb, size, cols)
            piece = lambda bits: take(held, links.b ^ bits, 0)
            self.near = jnp.stack([piece(0), piece(2)])
            sent = jnp.stack([piece(1), piece(3)]).astype(BF16)
        else:
            self.near, sent = pl.pallas_call(
                functools.partial(third_kernel, size),
                grid=(1,),
                in_specs=[SM, self.pick(0), self.pick(0), self.whole(self.block, cols)],
                out_specs=[self.whole(2, size, cols)] * 2,
                out_shape=[shape(2, size, cols, dtype=F32), shape(2, size, cols)],
                scratch_shapes=[pltpu.VMEM((self.block, cols), F32)],
                cost_estimate=cost(3),
                name="third",
            )(scalar(links.b), keep, self.got, self.more)
        self.near_got = links.flip_band(sent, 1)
        return sent

    def fourth(self, *deps):
        dims = (self.size, self.cols)
        pick = pl.BlockSpec((1,) + dims, lambda _: (1, 0, 0))
        sent = pl.pallas_call(
            second_kernel,
            grid=(1,),
            in_specs=[pick] * 2,
            out_specs=self.whole(*dims),
            out_shape=shape(*dims),
            cost_estimate=cost(2),
            name="fourth",
        )(after(self.near, *deps), self.near_got)
        self.far_got = self.links.flip_band(sent, 2)
        return sent

    def last(self, *deps):
        dims = (self.size, self.cols)
        pick = pl.BlockSpec((1,) + dims, lambda _: (0, 0, 0))
        return pl.pallas_call(
            functools.partial(last_kernel, self.widths),
            grid=(1,),
            in_specs=[pick, pick, self.whole(*dims)],
            out_specs=[self.whole(self.size, w) for w in self.widths],
            out_shape=[shape(self.size, w, dtype=F32) for w in self.widths],
            cost_estimate=cost(2),
            name="last",
        )(after(self.near, *deps), self.near_got, self.far_got)


class Table:
    def __init__(self, links, keep, send):
        self.links, self.keep, self.send = links, keep, send

    def start(self, *deps):
        self.got = self.links.flip(after(self.send, *deps), 1)

    def core(self, *deps):
        links = self.links
        x = links.by_quarter(after(self.keep, *deps) + self.got)
        x = x.reshape(2, 2, -1, x.shape[1])
        self.keep = take(x, links.p, 1)
        self.send = take(x, 1 - links.p, 1)
        self.got = links.flip(self.send, 2)
        return self.send

    def near(self, *deps):
        links = self.links
        x = after(self.keep, *deps) + self.got
        self.keep = take(x, links.q, 0)
        self.send = take(x, 1 - links.q, 0)
        self.got = links.flip(self.send, 4)
        return self.send

    def band(self, *deps):
        links, nb = self.links, self.links.nb
        x = links.sum_hi(after(self.keep, *deps) + self.got)
        x = x.reshape(2, 2, -1, x.shape[1])
        low, high = links.b & 1, links.b >> 1
        self.keep = take(x, low, 1)
        self.send = take(x, 1 - low, 1)
        self.got = links.flip_band(self.send, 1)
        return self.send

    def far(self, *deps):
        high = self.links.b >> 1
        x = after(self.keep, *deps) + self.got
        self.keep = take(x, high, 0)
        self.send = take(x, 1 - high, 0)
        self.got = self.links.flip_band(self.send, 2)
        return self.send

    def last(self, *deps):
        return after(self.keep, *deps) + self.got


def per_device(
    inputs, keep_mask, crop_rows, crop_cols, gain_one, shift_one, w_query, b_query, w_key, w_value,
    b_value, w_out, b_out, gain_two, shift_two, w_up, b_up, w_down, b_down, cotangent, *, n_img, nb,
):
    images, rows, width = inputs.shape
    hidden_width = w_up.shape[1]
    assert images == nb and nb == 4
    tokens = nb * rows
    links = Links(n_img, nb)
    core, band = scalar(links.c), scalar(links.b)
    f = lambda v: v.astype(F32)

    blocks = pl.pallas_call(
        functools.partial(spread_kernel, rows, nb),
        in_specs=[SM] * 3 + [VM] * 2,
        out_specs=[VM] * nb,
        out_shape=[shape(rows + 8, width)] * nb,
        cost_estimate=cost(2),
        name="spread",
    )(band, crop_rows, crop_cols, inputs, keep_mask)
    slots = [blocks[0]] + [links.band_shift(blocks[s], s) for s in range(1, nb)]
    given = after(cotangent, *blocks)
    cots = [take(given, links.b, 0)]
    for s in range(1, nb):
        cots.append(links.band_shift(take(given, (links.b + s) % nb, 0), s))
    vec = jnp.stack([f(t) for t in (gain_one, shift_one, b_query, b_value, b_out, gain_two, shift_two, b_down)])
    b_up_row = f(b_up)[None, :]

    block = width // (links.hi * 8)
    aligned = block % 16 == 0
    up_block = hidden_width // (links.hi * 8)
    half = width // 2
    full = shape(tokens, width)
    left_keep, left_send, q, k, v, middle, two, mask = pl.pallas_call(
        functools.partial(attend_kernel, rows, nb, block if aligned else half),
        in_specs=[SM] + [VM] * (nb + 5),
        out_specs=[VM] * 8,
        out_shape=[shape(3 * half, tokens)] * 2 + [full] * 3
        + [shape(tokens, width, dtype=F32), full, shape(8, tokens, dtype=F32)],
        scratch_shapes=[pltpu.VMEM((tokens, width), BF16), pltpu.VMEM((width, tokens), BF16)],
        cost_estimate=cost(9),
        name="attend",
    )(core if aligned else jnp.zeros_like(core), *slots, vec, w_query, w_key, w_value, w_out)
    third_of = lambda x, i: x[i * half : (i + 1) * half, :]
    if not aligned:
        pairs = [links.reclass(third_of(left_keep, i), third_of(left_send, i), block) for i in range(3)]
        left_keep, left_send = (jnp.concatenate(x, axis=0) for x in zip(*pairs))
    left_got = links.flip(left_send, 1)

    steps = 4
    wide = hidden_width // steps
    fixed = lambda *dims: pl.BlockSpec(dims, lambda j, *_: (0,) * len(dims))
    tall = lambda *dims: pl.BlockSpec(dims, lambda j, *_: (0, j))
    up = pl.pallas_call(
        functools.partial(up_kernel, rows, nb, steps, up_block),
        grid_spec=pltpu.PrefetchScalarGridSpec(
            num_scalar_prefetch=1,
            grid=(steps,),
            in_specs=[
                fixed(tokens, width), fixed(tokens, width), fixed(8, tokens), fixed(8, width),
                tall(width, wide), tall(1, wide),
                pl.BlockSpec((wide, width), lambda j, c: (j, 0)),
            ] + [fixed(rows, width)] * nb,
            out_specs=[pl.BlockSpec((wide // 2, tokens), lambda j, c: (j, 0))] * 2
            + [fixed(tokens, width + hidden_width), tall(8, wide)]
            + [fixed(rows, width)] * nb,
            scratch_shapes=[pltpu.VMEM((tokens, width), F32)],
        ),
        out_shape=[shape(hidden_width // 2, tokens)] * 2
        + [shape(tokens, width + hidden_width), shape(8, hidden_width, dtype=F32)]
        + [shape(rows, width)] * nb,
        cost_estimate=cost(10),
        name="up",
    )(core, two, middle, mask, vec, w_up, b_up_row, w_down, *cots)
    act_keep, act_send, right, up_sums = up[:4]
    act_got = links.flip(act_send, 1)
    right_got = links.flip(right, 1)
    out_blocks = [up[4]] + [links.band_shift(up[4 + s], -s) for s in range(1, nb)]

    grad_middle, grad_branch, down_sums = pl.pallas_call(
        functools.partial(down_kernel, rows, nb, steps),
        grid=(steps,),
        in_specs=[
            fixed(tokens, width), pl.BlockSpec((tokens, wide), lambda j: (0, j + width // wide)), tall(width, wide),
            fixed(tokens, width), fixed(8, tokens), fixed(8, width),
        ] + [fixed(rows, width)] * nb,
        out_specs=[fixed(tokens, width), fixed(tokens, width), fixed(8, width)],
        out_shape=[shape(tokens, width, dtype=F32), full, shape(8, width, dtype=F32)],
        scratch_shapes=[pltpu.VMEM((tokens, width), F32)],
        cost_estimate=cost(7),
        name="down",
    )(right, right, w_up, after(middle, left_got), mask, vec, *cots)
    branch_got = links.flip(grad_branch, 1)

    unit_down = Unit(
        links, hidden_width // 2,
        [(after(act_keep, grad_branch), act_got, 0, [(width, right, 0, right_got, 0)])],
    )
    low = lambda: pltpu.VMEM((width, tokens), BF16)
    back_right, attend_sums = pl.pallas_call(
        attend_back_kernel,
        in_specs=[VM] * 6,
        out_specs=[VM] * 2,
        out_shape=[shape(tokens, 3 * width), shape(8, width, dtype=F32)],
        scratch_shapes=[
            pltpu.VMEM((tokens, width), BF16), pltpu.VMEM((tokens, width), BF16), low(), low(), low(), low(),
            pltpu.VMEM((width, tokens), F32), pltpu.VMEM((width, tokens), F32),
        ],
        cost_estimate=cost(11),
        name="attend_back",
    )(after(grad_branch, unit_down.send), q, k, v, mask, w_out)
    back_got = links.flip(back_right, 1)

    mark = unit_down.second(back_right)
    unit_up = Unit(
        links, half,
        [
            (
                after(left_keep, mark, *out_blocks), left_got, 2,
                [(width, right, 1 + i, right_got, 1 + i) for i in range(hidden_width // width)],
            ),
            (left_keep, left_got, 1, [(width, grad_branch, 0, branch_got, 0)]),
        ],
    )
    mark = unit_down.third(unit_up.send)
    unit_qkv = Unit(
        links, half,
        [(after(left_keep, mark), left_got, 0, [(width, back_right, i, back_got, i) for i in range(3)])],
    )

    back = pl.pallas_call(
        functools.partial(input_back_kernel, rows, nb, block if aligned else half),
        in_specs=[SM] + [VM] * (nb + 8),
        out_specs=[VM] * (nb + 2),
        out_shape=[shape(rows, width)] * nb + [shape(half, COLS, dtype=F32)] * 2,
        cost_estimate=cost(5),
        name="input_back",
    )(
        core if aligned else jnp.zeros_like(core),
        *slots, after(back_right, unit_qkv.send), w_query, w_key, w_value, grad_middle, vec, down_sums, attend_sums,
    )
    table_pair = back[nb:]
    if not aligned:
        table_pair = links.reclass(*table_pair, block)
    grad_blocks = [back[0]] + [links.band_shift(back[s], -s) for s in range(1, nb)]
    mark = unit_down.fourth(back[0])
    mark = unit_up.second(mark)
    mark = unit_qkv.second(mark)
    up_cols = after(up_sums, mark)[0].reshape(width, hidden_width // width)
    up_cols = jnp.pad(up_cols, ((0, 0), (18, COLS - 18 - hidden_width // width))).reshape(-1, 2, block, COLS)
    class_of = lambda c: take(up_cols, c, 1).reshape(half, COLS)
    table = Table(links, table_pair[0] + class_of(links.c), table_pair[1] + class_of(1 - links.c))
    table.start()
    mark = unit_up.third(mark)
    mark = table.core(mark)
    mark = unit_qkv.third(mark)
    mark = table.near(mark)
    (g_w_down,) = unit_down.last(mark, *grad_blocks)
    mark = table.band(g_w_down)
    mark = unit_up.fourth(mark)
    mark = table.far(mark)
    mark = unit_qkv.fourth(mark)
    output, grad_inputs = pl.pallas_call(
        functools.partial(gather_kernel, nb),
        in_specs=[SM] + [VM] * (2 * nb),
        out_specs=[VM] * 2,
        out_shape=[shape(nb, rows, width), shape(nb, rows, width, dtype=F32)],
        cost_estimate=cost(2),
        name="gather",
    )(after(band, mark), *out_blocks, *grad_blocks)
    cols = table.last(output)
    unit_up.widths = [hidden_width, width]
    g_w_up, g_w_out = unit_up.last(cols)
    g_w_query, g_w_key, g_w_value = unit_qkv.last(g_w_up)
    sums = [cols[:, i] for i in range(18)]
    g_b_up = cols[:, 18 : 18 + hidden_width // width].reshape(-1)
    return (
        output,
        grad_inputs,
        sums[16],
        sums[17],
        g_w_query,
        sums[8],
        g_w_key,
        g_w_value,
        sums[9],
        g_w_out,
        sums[2],
        sums[0],
        sums[1],
        g_w_up,
        g_b_up,
        g_w_down,
        sums[3],
    )


def solution(mesh):
    n_img, nb = mesh.shape["img"], mesh.shape["band"]

    def body(*args):
        return per_device(*args, n_img=n_img, nb=nb)

    both = P(("img", "band"))
    rows = P(("img", "band"), None)
    token = P("img", "band", None)
    return jax.shard_map(
        body,
        mesh=mesh,
        in_specs=(token, P("img", "band"), P("img"), P("img")) + (P(),) * 15 + (token,),
        out_specs=(
            token, token, both, both, rows, both, rows, rows, both, rows, both, both, both, rows, both,
            rows, both,
        ),
        check_vma=False,
    )
```

```python
import functools

import jax
import jax.numpy as jnp
from jax import lax
from jax.experimental import pallas as pl
from jax.experimental.pallas import tpu as pltpu
from jax.sharding import PartitionSpec as P

HEADS = 16
HEAD_DIM = 48
SIDE = 16
EPS = 1e-05
F32 = jnp.float32
BF16 = jnp.bfloat16
GROUP = 8
GROUP_LANES = GROUP * HEAD_DIM
SCALE = HEAD_DIM ** (-0.5)


def dot_nn(a, b):
    return lax.dot_general(a, b, (((1,), (0,)), ((), ())), preferred_element_type=F32)


def dot_nt(a, b):
    return lax.dot_general(a, b, (((1,), (1,)), ((), ())), preferred_element_type=F32)


def dot_tn(a, b):
    return lax.dot_general(a, b, (((0,), (0,)), ((), ())), preferred_element_type=F32)


def norm_stats(x):
    mean = jnp.mean(x, axis=-1, keepdims=True)
    centred = x - mean
    var = jnp.mean(centred * centred, axis=-1, keepdims=True)
    r = lax.rsqrt(var + EPS)
    return centred * r, r


def norm_back(grad, n, r, gain):
    e = grad * gain
    return r * (e - jnp.mean(e, axis=-1, keepdims=True) - n * jnp.mean(e * n, axis=-1, keepdims=True))


def colsum(x):
    return jnp.sum(x.astype(F32), axis=0, keepdims=True)


def take(x, index, axis):
    return lax.dynamic_index_in_dim(x, index, axis, keepdims=False)


GAIN1, SHIFT1, BQ, BV, BO, GAIN2, SHIFT2, BDOWN = range(8)


def windows():
    out = []
    for h in range(GROUP):
        first, last = h * HEAD_DIM, (h + 1) * HEAD_DIM
        lo, hi = first // 128 * 128, -(-last // 128) * 128
        out.append((lo, hi, first - lo, last - lo))
    return out


def head_lanes(shape, first, last):
    lane = lax.broadcasted_iota(jnp.int32, shape, 1)
    return (lane >= first) & (lane < last)


def turn(x):
    return jnp.transpose(x.astype(F32)).astype(BF16)


def split_rows(x, block, c, keep, send, at=0):
    for i in range(x.shape[0] // (2 * block)):
        even, odd = x[2 * i * block : (2 * i + 1) * block, :], x[(2 * i + 1) * block : (2 * i + 2) * block, :]
        rows = pl.ds(at + i * block, block)
        keep[rows, :] = jnp.where(c == 0, even, odd)
        send[rows, :] = jnp.where(c == 0, odd, even)


def join(refs, rows):
    return jnp.concatenate([r[:rows, :] for r in refs], axis=0)


def column_of(row):
    n = row.shape[1]
    eye = lax.broadcasted_iota(jnp.int32, (n, n), 0) == lax.broadcasted_iota(jnp.int32, (n, n), 1)
    return jnp.sum(jnp.where(eye, row, 0.0), axis=1, keepdims=True)


def attend_kernel(rows, nb, block, core, *refs):
    slots = refs[:nb]
    c = core[0]
    vec, wq, wk, wv, wo = refs[nb : nb + 5]
    keep_o, send_o, q_o, k_o, v_o, mid_o, two_o, mask_o, att_o, kt = refs[nb + 5 :]
    tokens = nb * rows
    half = q_o.shape[1] // 2
    row = jnp.zeros((1, tokens), F32)
    for s in range(nb):
        row = row + slots[s][rows : rows + 8, :tokens].astype(F32)[s : s + 1, :]
    mask_o[...] = jnp.broadcast_to(row, mask_o.shape)
    x = join(slots, rows).astype(F32)
    n1, _ = norm_stats(x)
    normed = (n1 * vec[GAIN1 : GAIN1 + 1, :] + vec[SHIFT1 : SHIFT1 + 1, :]).astype(BF16)
    split_rows(turn(normed), block, c, keep_o, send_o)
    q_o[...] = (dot_nn(normed, wq[...]) + vec[BQ : BQ + 1, :]).astype(BF16)
    k = dot_nn(normed, wk[...]).astype(BF16)
    k_o[...] = k
    kt[...] = turn(k)
    v_o[...] = (dot_nn(normed, wv[...]) + vec[BV : BV + 1, :]).astype(BF16)
    keep = row > 0.5

    def group(g, carry):
        base = pl.multiple_of(g * GROUP_LANES, 128)
        blocks = [jnp.zeros((tokens, 128), F32) for _ in range(GROUP_LANES // 128)]
        for lo, hi, first, last in windows():
            wide = hi - lo
            here = head_lanes((tokens, wide), first, last)
            at = pl.ds(base + lo, wide)
            zero = jnp.zeros((tokens, wide), BF16)
            qm = jnp.where(here, q_o[:, at], zero)
            s = dot_nn(qm, kt[at, :]) * SCALE
            s = jnp.where(keep, s, -1e30)
            e = jnp.exp(s - jnp.max(s, axis=-1, keepdims=True))
            p = (e * (1.0 / jnp.sum(e, axis=-1, keepdims=True))).astype(BF16)
            o = dot_nn(p, jnp.where(here, v_o[:, at], zero))
            for j in range(wide // 128):
                blocks[lo // 128 + j] = blocks[lo // 128 + j] + o[:, j * 128 : (j + 1) * 128]
        att_o[:, pl.ds(base, GROUP_LANES)] = jnp.concatenate(blocks, axis=1).astype(BF16)
        return carry

    lax.fori_loop(0, HEADS // GROUP, group, 0)
    split_rows(turn(att_o[...]), block, c, keep_o, send_o, half)
    middle = x + (dot_nn(att_o[...], wo[...]) + vec[BO : BO + 1, :])
    mid_o[...] = middle
    n2, _ = norm_stats(middle)
    two = (n2 * vec[GAIN2 : GAIN2 + 1, :] + vec[SHIFT2 : SHIFT2 + 1, :]).astype(BF16)
    two_o[...] = two
    split_rows(turn(two), block, c, keep_o, send_o, 2 * half)


def up_kernel(rows, nb, steps, block, core, *refs):
    two, middle, mask, vec, w_up, b_up, w_down = refs[:7]
    cots = refs[7 : 7 + nb]
    act_keep, act_send, right_o, bsum = refs[7 + nb : 11 + nb]
    out_o, acc = refs[11 + nb :]
    j = pl.program_id(0)
    width = acc.shape[1]

    @pl.when(j == 0)
    def _():
        col = column_of(mask[0:1, :])
        right_o[:, :width] = (join(cots, rows).astype(F32) * col).astype(BF16)

    hidden = dot_nn(two[...], w_up[...]) + b_up[0:1, :]
    cdf = 0.5 * (1.0 + lax.erf(hidden * 0.7071067811865476))
    pdf = jnp.exp(-0.5 * hidden * hidden) * 0.3989422804014327
    act = (hidden * cdf).astype(BF16)
    split_rows(turn(act), block, core[0], act_keep, act_send)
    part = dot_nn(act, w_down[...])
    acc[...] = jnp.where(j == 0, part, acc[...] + part)
    gh = (dot_nt(right_o[:, :width], w_down[...]) * (cdf + hidden * pdf)).astype(BF16)
    right_o[:, pl.ds(pl.multiple_of(width + j * gh.shape[1], 128), gh.shape[1])] = gh
    bsum[...] = jnp.broadcast_to(colsum(gh), bsum.shape)

    @pl.when(j == steps - 1)
    def _():
        col = column_of(mask[0:1, :])
        out_o[...] = (col * (middle[...] + (acc[...] + vec[BDOWN : BDOWN + 1, :]))).astype(BF16)


def down_kernel(rows, nb, steps, *refs):
    gd, gh, w_up, middle, mask, vec = refs[:6]
    cots = refs[6 : 6 + nb]
    gm_o, gb_o, sums, acc = refs[6 + nb :]
    j = pl.program_id(0)
    part = dot_nt(gh[...], w_up[...])
    acc[...] = jnp.where(j == 0, part, acc[...] + part)

    @pl.when(j == steps - 1)
    def _():
        grad = acc[...]
        n2, r2 = norm_stats(middle[...])
        col = column_of(mask[0:1, :])
        result = join(cots, rows).astype(F32) * col
        gm = result + norm_back(grad, n2, r2, vec[GAIN2 : GAIN2 + 1, :])
        gm_o[...] = gm
        gb = gm.astype(BF16)
        gb_o[...] = gb
        sums[0:1, :] = colsum(grad * n2)
        sums[1:2, :] = colsum(grad)
        sums[2:3, :] = colsum(gb)
        sums[3:4, :] = colsum(gd[...])
        sums[4:8, :] = jnp.zeros((4, sums.shape[1]), F32)


def attend_back_kernel(gb, q, k, v, mask, wo, right_o, sums, gq_o, ga, qt, kt, vt, gat, gkt, gvt):
    tokens, width = gb.shape
    g_att = dot_nt(gb[...], wo[...]).astype(BF16)
    ga[...] = g_att
    gat[...] = turn(g_att)
    qt[...] = turn(q[...])
    kt[...] = turn(k[...])
    vt[...] = turn(v[...])
    keep = mask[0:1, :] > 0.5

    def group(g, carry):
        base = pl.multiple_of(g * GROUP_LANES, 128)
        blocks = [jnp.zeros((tokens, 128), F32) for _ in range(GROUP_LANES // 128)]
        for h, (lo, hi, first, last) in enumerate(windows()):
            wide = hi - lo
            here = head_lanes((tokens, wide), first, last)
            at = pl.ds(base + lo, wide)
            own = pl.ds(pl.multiple_of(base + h * HEAD_DIM, 16), HEAD_DIM)
            zero = jnp.zeros((tokens, wide), BF16)
            s = dot_nn(jnp.where(here, q[:, at], zero), kt[at, :]) * SCALE
            s = jnp.where(keep, s, -1e30)
            e = jnp.exp(s - jnp.max(s, axis=-1, keepdims=True))
            p = e * (1.0 / jnp.sum(e, axis=-1, keepdims=True))
            dp = dot_nn(jnp.where(here, ga[:, at], zero), vt[at, :])
            gvt[own, :] = dot_nn(gat[own, :], p.astype(BF16))
            ds = (p * (dp - jnp.sum(p * dp, axis=-1, keepdims=True))).astype(BF16)
            gkt[own, :] = dot_nn(qt[own, :], ds)
            o = dot_nn(ds, jnp.where(here, k[:, at], zero))
            for j in range(wide // 128):
                blocks[lo // 128 + j] = blocks[lo // 128 + j] + o[:, j * 128 : (j + 1) * 128]
        gq_o[:, pl.ds(base, GROUP_LANES)] = (jnp.concatenate(blocks, axis=1) * SCALE).astype(BF16)
        return carry

    lax.fori_loop(0, HEADS // GROUP, group, 0)
    gq = gq_o[...]
    gk = (jnp.transpose(gkt[...]) * SCALE).astype(BF16)
    gv = jnp.transpose(gvt[...]).astype(BF16)
    for i, t in enumerate((gq, gk, gv)):
        right_o[:, i * width : (i + 1) * width] = t
    sums[0:1, :] = colsum(gq)
    sums[1:2, :] = colsum(gv)
    sums[2:8, :] = jnp.zeros((6, width), F32)


def input_back_kernel(rows, nb, block, core, band, *refs):
    slots = refs[:nb]
    right, wq, wk, wv, gm, vec, down_sums, attend_sums, up_cols = refs[nb : nb + 9]
    result, own_o, near_o, far_o, keep_o, send_o, held = refs[nb + 9 :]
    width = gm.shape[1]
    grad = dot_nt(right[:, :width], wq[...])
    grad = grad + dot_nt(right[:, width : 2 * width], wk[...])
    grad = grad + dot_nt(right[:, 2 * width :], wv[...])
    n1, r1 = norm_stats(join(slots, rows).astype(F32))
    gx = (gm[...] + norm_back(grad, n1, r1, vec[GAIN1 : GAIN1 + 1, :])).astype(BF16)
    held[...] = gx
    for bits, out, at in ((0, own_o, 0), (1, near_o, 0), (3, near_o, 2 * rows), (2, far_o, 0)):
        slot = lax.rem(band[0] - jnp.bitwise_xor(band[0], bits) + nb, nb)
        tokens = pl.ds(pl.multiple_of(slot * rows, 16), rows)
        out[at : at + rows, :] = result[tokens, :]
        out[at + rows : at + 2 * rows, :] = held[tokens, :]
    table = jnp.concatenate(
        [
            down_sums[...], attend_sums[...], colsum(grad * n1), colsum(grad),
            jnp.zeros((COLS - 18, width), F32),
        ],
        axis=0,
    )
    split_rows(jnp.transpose(table) + up_cols[...], block, core[0], keep_o, send_o)


def spread_kernel(rows, nb, band, crop_rows, crop_cols, x, keep_mask, *outs):
    width = x.shape[2]
    position = band[0] * rows + lax.broadcasted_iota(jnp.int32, (1, rows), 1)
    slot = lax.broadcasted_iota(jnp.int32, (8, width), 0)
    lane = lax.broadcasted_iota(jnp.int32, (8, width), 1) // rows
    for s in range(nb):
        image = lax.rem(band[0] + s, nb)
        outs[s][:rows, :] = x[image]
        inside = (
            (keep_mask[pl.ds(image, 1), :] > 0)
            & (position // SIDE < crop_rows[image])
            & (position % SIDE < crop_cols[image])
        )
        flags = jnp.concatenate([jnp.where(inside, 1.0, 0.0)] * (width // rows), axis=1)
        outs[s][rows:, :] = jnp.where((slot == s) & (lane == s), flags, 0.0).astype(BF16)


def gather_kernel(band, own, near, far, output, grad):
    rows = output.shape[1]
    for bits, ref, at in ((0, own, 0), (1, near, 0), (2, far, 0), (3, far, 2 * rows)):
        image = jnp.bitwise_xor(band[0], bits)
        output[image] = ref[at : at + rows, :]
        grad[image] = ref[at + rows : at + 2 * rows, :].astype(F32)


def weight_kernel(groups, extra, quarters, *refs):
    t = pl.program_id(0)
    parts, at = [], 0
    for widths in groups:
        left, left_got = refs[at : at + 2]
        at += 2
        for _ in widths:
            right, right_got = refs[at : at + 2]
            at += 2
            parts.append((dot_nn(left[...], right[...]) + dot_nn(left_got[...], right_got[...])).astype(BF16))
    if extra:
        parts.append((refs[at][...] + refs[at + 1][...]).astype(BF16))
        at += 2
    send, keep = refs[at:]
    g = parts[0] if len(parts) == 1 else jnp.concatenate(parts, axis=1)

    @pl.when(t < 2)
    def _():
        send[0] = g

    @pl.when(t >= 2)
    def _():
        keep[0] = g


def second_kernel(keep, got, out):
    out[...] = (keep[0].astype(F32) + got[0].astype(F32)).astype(BF16)


def third_kernel(size, band, keep, got, more, keep_o, send_o, held):
    held[...] = keep[0].astype(F32) + got[0].astype(F32) + more[...].astype(F32)
    for i in range(2):
        near = jnp.bitwise_xor(band[0], 2 * i)
        far = jnp.bitwise_xor(band[0], 2 * i + 1)
        keep_o[i] = held[pl.ds(pl.multiple_of(near * size, 8), size), :]
        send_o[i] = held[pl.ds(pl.multiple_of(far * size, 8), size), :].astype(BF16)


def last_kernel(widths, vectors, keep, got, more, *outs):
    at = 0
    for w, out in zip(widths, outs):
        cols = pl.ds(at, w)
        out[...] = keep[0, :, cols] + got[0, :, cols].astype(F32) + more[:, cols].astype(F32)
        at += w
    if vectors:
        cols = pl.ds(at, COLS)
        table = jnp.transpose(keep[0, :, cols] + got[0, :, cols].astype(F32) + more[:, cols].astype(F32))
        for (first, n), out in zip(vectors, outs[len(widths) :]):
            out[...] = jnp.concatenate([table[first + i : first + i + 1, :] for i in range(n)], axis=1)


COLS = 128
LIMIT = pltpu.CompilerParams(vmem_limit_bytes=20 * 1024 * 1024)
USED = (16, 17, 8, 9, 2, 0, 1, 3)


VM = pl.BlockSpec(memory_space=pltpu.VMEM)
SM = pl.BlockSpec(memory_space=pltpu.SMEM)


def shape(*dims, dtype=BF16):
    return jax.ShapeDtypeStruct(dims, dtype)


def cost(us):
    return pl.CostEstimate(flops=int(us * 2500000000), bytes_accessed=int(us * 10000000), transcendentals=0)


def after(x, *others):
    return lax.optimization_barrier((x, others))[0]


def scalar(x):
    return x.astype(jnp.int32).reshape(1)


class Links:
    def __init__(self, n_img, n_band):
        self.n_img, self.nb = n_img, n_band
        self.hi = n_img // 8
        i = lax.axis_index("img")
        self.c = i & 1
        self.p = (i >> 1) & 1
        self.q = (i >> 2) & 1
        self.h = i >> 3
        self.b = lax.axis_index("band")

    def flip(self, x, bit):
        return lax.ppermute(x, "img", [(k, k ^ bit) for k in range(self.n_img)])

    def flip_by_core(self, x, even, odd):
        return lax.ppermute(x, "img", [(k, k ^ (odd if k & 1 else even)) for k in range(self.n_img)])

    def flip_band(self, x, bit):
        return lax.ppermute(x, "band", [(k, k ^ bit) for k in range(self.nb)])

    def band_shift(self, x, s):
        return lax.ppermute(x, "band", [(k, (k + s) % self.nb) for k in range(self.nb)])

    def hi_shift(self, x, s):
        n = self.n_img
        return lax.ppermute(x, "img", [(k, (k + 8 * s) % n) for k in range(n)])

    def sum_hi(self, x):
        x = x.reshape(self.hi, x.shape[0] // self.hi, *x.shape[1:])
        total = take(x, self.h, 0)
        for s in range(1, self.hi):
            total = total + self.hi_shift(take(x, (self.h + s) % self.hi, 0).astype(BF16), s).astype(F32)
        return total

    def by_quarter(self, x):
        if self.hi == 1:
            return x
        return x.reshape(self.hi, 4, -1, x.shape[1]).swapaxes(0, 1).reshape(x.shape)

    def reclass(self, first, second, block):
        x = jnp.concatenate([first, second], axis=0)
        x = x.reshape(-1, 2, block, x.shape[1])
        own, other = take(x, self.c, 1), take(x, 1 - self.c, 1)
        return own.reshape(-1, x.shape[3]), other.reshape(-1, x.shape[3])


class Unit:
    def __init__(self, links, rows, groups, extra=()):
        self.links, self.vectors = links, []
        args, specs, widths = [], [], []
        tokens = groups[0][0].shape[1]
        self.block = block = rows // 4
        for left, left_got, left_at, rights in groups:
            if links.hi > 1:
                left, left_got = (x[left_at * rows : (left_at + 1) * rows, :] for x in (left, left_got))
                left_at = 0
            args += [links.by_quarter(left), links.by_quarter(left_got)]
            specs += [pl.BlockSpec((block, tokens), lambda t, s, i=4 * left_at: (s[t] + i, 0))] * 2
            widths.append([w for w, _, _, _, _ in rights])
            for w, own, own_at, got, got_at in rights:
                args += [own, got]
                specs.append(pl.BlockSpec((tokens, w), lambda t, s, i=own_at: (0, i)))
                specs.append(pl.BlockSpec((tokens, w), lambda t, s, i=got_at: (0, i)))
        for x in extra:
            args.append(links.by_quarter(x))
            specs.append(pl.BlockSpec((block, COLS), lambda t, s: (s[t], 0)))
        self.extra = len(extra) > 0
        self.widths = [w for ws in widths for w in ws] + [COLS] * self.extra
        self.cols = cols = sum(self.widths)
        p, q = links.p, links.q
        even = links.c == 0
        at = lambda a, b: a * 2 + b
        quarters = jnp.stack(
            [
                jnp.where(even, at(q, 1 - p), at(1 - q, p)), at(1 - q, 1 - p),
                jnp.where(even, at(1 - q, p), at(q, 1 - p)), at(q, p),
            ]
        ).astype(jnp.int32)
        one = lambda x: jnp.asarray(x).astype(jnp.int32)
        self.send, self.keep = pl.pallas_call(
            functools.partial(weight_kernel, widths, self.extra),
            grid_spec=pltpu.PrefetchScalarGridSpec(
                num_scalar_prefetch=1,
                grid=(4,),
                in_specs=specs,
                out_specs=[
                    pl.BlockSpec((1, block, cols), lambda t, s: (one(t > 0), 0, 0)),
                    pl.BlockSpec((1, block, cols), lambda t, s: (one(t < 3), 0, 0)),
                ],
            ),
            out_shape=[shape(2, block, cols)] * 2,
            cost_estimate=cost(0.1 if extra else 6),
            compiler_params=LIMIT,
            name="weight_grad",
        )(quarters, *args)
        self.got = links.flip_by_core(self.send, 2, 4)

    def pick(self, i):
        return pl.BlockSpec((1, self.block, self.cols), lambda _: (i, 0, 0))

    def whole(self, *dims):
        return pl.BlockSpec(dims, lambda _: (0,) * len(dims))

    def second(self, *deps):
        dims = (self.block, self.cols)
        sent = pl.pallas_call(
            second_kernel,
            grid=(1,),
            in_specs=[self.pick(1)] * 2,
            out_specs=self.whole(*dims),
            out_shape=shape(*dims),
            cost_estimate=cost(2),
            compiler_params=LIMIT,
            name="second",
        )(after(self.keep, *deps), self.got)
        self.more = self.links.flip_by_core(sent, 4, 2)
        return sent

    def third(self, *deps):
        links, nb, cols = self.links, self.links.nb, self.cols
        self.size = size = self.block // (links.hi * nb)
        keep = after(self.keep, *deps)
        if links.hi > 1 or size % 8:
            held = links.sum_hi(keep[0].astype(F32) + self.got[0].astype(F32) + self.more.astype(F32))
            held = held.reshape(nb, size, cols)
            piece = lambda bits: take(held, links.b ^ bits, 0)
            self.near = jnp.stack([piece(0), piece(2)])
            sent = jnp.stack([piece(1), piece(3)]).astype(BF16)
        else:
            self.near, sent = pl.pallas_call(
                functools.partial(third_kernel, size),
                grid=(1,),
                in_specs=[SM, self.pick(0), self.pick(0), self.whole(self.block, cols)],
                out_specs=[self.whole(2, size, cols)] * 2,
                out_shape=[shape(2, size, cols, dtype=F32), shape(2, size, cols)],
                scratch_shapes=[pltpu.VMEM((self.block, cols), F32)],
                cost_estimate=cost(3),
                compiler_params=LIMIT,
                name="third",
            )(scalar(links.b), keep, self.got, self.more)
        self.near_got = links.flip_band(sent, 1)
        return sent

    def fourth(self, *deps):
        dims = (self.size, self.cols)
        pick = pl.BlockSpec((1,) + dims, lambda _: (1, 0, 0))
        sent = pl.pallas_call(
            second_kernel,
            grid=(1,),
            in_specs=[pick] * 2,
            out_specs=self.whole(*dims),
            out_shape=shape(*dims),
            cost_estimate=cost(2),
            compiler_params=LIMIT,
            name="fourth",
        )(after(self.near, *deps), self.near_got)
        self.far_got = self.links.flip_band(sent, 2)
        return sent

    def last(self, *deps):
        dims = (self.size, self.cols)
        pick = pl.BlockSpec((1,) + dims, lambda _: (0, 0, 0))
        vectors = self.vectors
        outs = [(self.size, w) for w in self.widths] + [(1, n * self.size) for _, n in vectors]
        return pl.pallas_call(
            functools.partial(last_kernel, self.widths, vectors),
            grid=(1,),
            in_specs=[pick, pick, self.whole(*dims)],
            out_specs=[self.whole(*d) for d in outs],
            out_shape=[shape(*d, dtype=F32) for d in outs],
            cost_estimate=cost(2),
            compiler_params=LIMIT,
            name="last",
        )(after(self.near, *deps), self.near_got, self.far_got)


def per_device(
    inputs, keep_mask, crop_rows, crop_cols, gain_one, shift_one, w_query, b_query, w_key, w_value,
    b_value, w_out, b_out, gain_two, shift_two, w_up, b_up, w_down, b_down, cotangent, *, n_img, nb,
):
    images, rows, width = inputs.shape
    hidden_width = w_up.shape[1]
    assert images == nb and nb == 4
    tokens = nb * rows
    links = Links(n_img, nb)
    core, band = scalar(links.c), scalar(links.b)
    f = lambda v: v.astype(F32)

    blocks = pl.pallas_call(
        functools.partial(spread_kernel, rows, nb),
        in_specs=[SM] * 3 + [VM] * 2,
        out_specs=[VM] * nb,
        out_shape=[shape(rows + 8, width)] * nb,
        cost_estimate=cost(2),
        name="spread",
    )(band, crop_rows, crop_cols, inputs, keep_mask)
    slots = [blocks[0]] + [links.band_shift(blocks[s], s) for s in range(1, nb)]
    given = after(cotangent, *blocks)
    cots = [take(given, links.b, 0)]
    for s in range(1, nb):
        cots.append(links.band_shift(take(given, (links.b + s) % nb, 0), s))
    vec = jnp.stack([f(t) for t in (gain_one, shift_one, b_query, b_value, b_out, gain_two, shift_two, b_down)])
    b_up_row = f(b_up)[None, :]

    block = width // (links.hi * 8)
    aligned = block % 16 == 0
    up_block = hidden_width // (links.hi * 8)
    half = width // 2
    full = shape(tokens, width)
    left_keep, left_send, q, k, v, middle, two, mask = pl.pallas_call(
        functools.partial(attend_kernel, rows, nb, block if aligned else half),
        in_specs=[SM] + [VM] * (nb + 5),
        out_specs=[VM] * 8,
        out_shape=[shape(3 * half, tokens)] * 2 + [full] * 3
        + [shape(tokens, width, dtype=F32), full, shape(8, tokens, dtype=F32)],
        scratch_shapes=[pltpu.VMEM((tokens, width), BF16), pltpu.VMEM((width, tokens), BF16)],
        cost_estimate=cost(9),
        name="attend",
    )(core if aligned else jnp.zeros_like(core), *slots, vec, w_query, w_key, w_value, w_out)
    third_of = lambda x, i: x[i * half : (i + 1) * half, :]
    if not aligned:
        pairs = [links.reclass(third_of(left_keep, i), third_of(left_send, i), block) for i in range(3)]
        left_keep, left_send = (jnp.concatenate(x, axis=0) for x in zip(*pairs))
    left_got = links.flip(left_send, 1)

    steps = 4
    wide = hidden_width // steps
    fixed = lambda *dims: pl.BlockSpec(dims, lambda j, *_: (0,) * len(dims))
    tall = lambda *dims: pl.BlockSpec(dims, lambda j, *_: (0, j))
    up = pl.pallas_call(
        functools.partial(up_kernel, rows, nb, steps, up_block),
        grid_spec=pltpu.PrefetchScalarGridSpec(
            num_scalar_prefetch=1,
            grid=(steps,),
            in_specs=[
                fixed(tokens, width), fixed(tokens, width), fixed(8, tokens), fixed(8, width),
                tall(width, wide), tall(1, wide),
                pl.BlockSpec((wide, width), lambda j, c: (j, 0)),
            ] + [fixed(rows, width)] * nb,
            out_specs=[pl.BlockSpec((wide // 2, tokens), lambda j, c: (j, 0))] * 2
            + [fixed(tokens, width + hidden_width), tall(8, wide), fixed(tokens, width)],
            scratch_shapes=[pltpu.VMEM((tokens, width), F32)],
        ),
        out_shape=[shape(hidden_width // 2, tokens)] * 2
        + [shape(tokens, width + hidden_width), shape(8, hidden_width, dtype=F32), full],
        cost_estimate=cost(10),
        name="up",
    )(core, two, middle, mask, vec, w_up, b_up_row, w_down, *cots)
    act_keep, act_send, right, up_sums, result = up
    act_got = links.flip(act_send, 1)
    right_got = links.flip(right, 1)

    grad_middle, grad_branch, down_sums = pl.pallas_call(
        functools.partial(down_kernel, rows, nb, steps),
        grid=(steps,),
        in_specs=[
            fixed(tokens, width), pl.BlockSpec((tokens, wide), lambda j: (0, j + width // wide)), tall(width, wide),
            fixed(tokens, width), fixed(8, tokens), fixed(8, width),
        ] + [fixed(rows, width)] * nb,
        out_specs=[fixed(tokens, width), fixed(tokens, width), fixed(8, width)],
        out_shape=[shape(tokens, width, dtype=F32), full, shape(8, width, dtype=F32)],
        scratch_shapes=[pltpu.VMEM((tokens, width), F32)],
        cost_estimate=cost(7),
        name="down",
    )(right, right, w_up, after(middle, left_got), mask, vec, *cots)
    branch_got = links.flip(grad_branch, 1)

    unit_down = Unit(
        links, hidden_width // 2,
        [(after(act_keep, grad_branch), act_got, 0, [(width, right, 0, right_got, 0)])],
    )
    unit_up = Unit(
        links, half,
        [
            (
                after(left_keep, unit_down.send), left_got, 2,
                [(width, right, 1 + i, right_got, 1 + i) for i in range(hidden_width // width)],
            ),
            (left_keep, left_got, 1, [(width, grad_branch, 0, branch_got, 0)]),
        ],
    )
    low = lambda: pltpu.VMEM((width, tokens), BF16)
    back_right, attend_sums = pl.pallas_call(
        attend_back_kernel,
        in_specs=[VM] * 6,
        out_specs=[VM] * 2,
        out_shape=[shape(tokens, 3 * width), shape(8, width, dtype=F32)],
        scratch_shapes=[
            pltpu.VMEM((tokens, width), BF16), pltpu.VMEM((tokens, width), BF16), low(), low(), low(), low(),
            pltpu.VMEM((width, tokens), F32), pltpu.VMEM((width, tokens), F32),
        ],
        cost_estimate=cost(11),
        compiler_params=LIMIT,
        name="attend_back",
    )(after(grad_branch, unit_up.send), q, k, v, mask, w_out)
    back_got = links.flip(back_right, 1)

    mark = unit_down.second(back_right)
    per_row = hidden_width // width
    up_cols = up_sums[0].reshape(n_img * nb, per_row, -1).swapaxes(1, 2).reshape(width, per_row)
    up_cols = jnp.pad(up_cols, ((0, 0), (18, COLS - 18 - per_row)))
    back = pl.pallas_call(
        functools.partial(input_back_kernel, rows, nb, block if aligned else half),
        in_specs=[SM] * 2 + [VM] * (nb + 10),
        out_specs=[VM] * 5,
        out_shape=[shape(2 * rows, width), shape(4 * rows, width), shape(2 * rows, width)]
        + [shape(half, COLS, dtype=F32)] * 2,
        scratch_shapes=[pltpu.VMEM((tokens, width), BF16)],
        cost_estimate=cost(5),
        compiler_params=LIMIT,
        name="input_back",
    )(
        core if aligned else jnp.zeros_like(core), band,
        *slots, after(back_right, mark), w_query, w_key, w_value, grad_middle, vec, down_sums, attend_sums, up_cols,
        result,
    )
    blocks, table = back[:3], back[3:]
    near_got = links.flip_band(blocks[1], 1)
    if not aligned:
        table = links.reclass(*table, block)
    table_got = links.flip(table[1], 1)

    unit_qkv = Unit(
        links, half,
        [(after(left_keep, blocks[0]), left_got, 0, [(width, back_right, i, back_got, i) for i in range(3)])],
        (table[0], table_got),
    )
    far_got = links.flip_band(jnp.concatenate([after(blocks[2], unit_qkv.send), near_got[2 * rows :, :]]), 2)
    mark = unit_up.second(unit_qkv.send)
    mark = unit_down.third(mark)
    mark = unit_qkv.second(mark)
    mark = unit_up.third(mark)
    mark = unit_down.fourth(mark)
    mark = unit_qkv.third(mark)
    mark = unit_up.fourth(mark)
    mark = unit_qkv.fourth(mark)
    (g_w_down,) = unit_down.last(mark)
    output, grad_inputs = pl.pallas_call(
        gather_kernel,
        in_specs=[SM] + [VM] * 3,
        out_specs=[VM] * 2,
        out_shape=[shape(nb, rows, width), shape(nb, rows, width, dtype=F32)],
        cost_estimate=cost(2),
        compiler_params=LIMIT,
        name="gather",
    )(after(band, g_w_down), blocks[0], near_got, far_got)
    mark = output
    unit_up.widths = [hidden_width, width]
    g_w_up, g_w_out = unit_up.last(mark)
    if unit_qkv.size % 8 == 0:
        unit_qkv.widths = [width] * 3
        unit_qkv.vectors = [(i, 1) for i in USED] + [(18, per_row)]
        g_w_query, g_w_key, g_w_value, *rest = unit_qkv.last(g_w_up)
        sums = {i: x[0] for i, x in zip(USED + (18,), rest)}
    else:
        g_w_query, g_w_key, g_w_value, cols = unit_qkv.last(g_w_up)
        sums = [cols[:, i] for i in range(18)] + [cols[:, 18 : 18 + per_row].swapaxes(0, 1).reshape(-1)]
    return (
        output,
        grad_inputs,
        sums[16],
        sums[17],
        g_w_query,
        sums[8],
        g_w_key,
        g_w_value,
        sums[9],
        g_w_out,
        sums[2],
        sums[0],
        sums[1],
        g_w_up,
        sums[18],
        g_w_down,
        sums[3],
    )


def solution(mesh):
    n_img, nb = mesh.shape["img"], mesh.shape["band"]

    def body(*args):
        return per_device(*args, n_img=n_img, nb=nb)

    both = P(("img", "band"))
    rows = P(("img", "band"), None)
    token = P("img", "band", None)
    return jax.shard_map(
        body,
        mesh=mesh,
        in_specs=(token, P("img", "band"), P("img"), P("img")) + (P(),) * 15 + (token,),
        out_specs=(
            token, token, both, both, rows, both, rows, rows, both, rows, both, both, both, rows, both,
            rows, both,
        ),
        check_vma=False,
    )
```

```python
import functools

import jax
import jax.numpy as jnp
from jax import lax
from jax.experimental import pallas as pl
from jax.experimental.pallas import tpu as pltpu
from jax.sharding import PartitionSpec as P

HEADS = 16
HEAD_DIM = 48
SIDE = 16
EPS = 1e-05
F32 = jnp.float32
BF16 = jnp.bfloat16
GROUP = 8
GROUP_LANES = GROUP * HEAD_DIM
SCALE = HEAD_DIM ** (-0.5)


def dot_nn(a, b):
    return lax.dot_general(a, b, (((1,), (0,)), ((), ())), preferred_element_type=F32)


def dot_nt(a, b):
    return lax.dot_general(a, b, (((1,), (1,)), ((), ())), preferred_element_type=F32)


def dot_tn(a, b):
    return lax.dot_general(a, b, (((0,), (0,)), ((), ())), preferred_element_type=F32)


def norm_stats(x):
    mean = jnp.mean(x, axis=-1, keepdims=True)
    centred = x - mean
    var = jnp.mean(centred * centred, axis=-1, keepdims=True)
    r = lax.rsqrt(var + EPS)
    return centred * r, r


def norm_back(grad, n, r, gain):
    e = grad * gain
    return r * (e - jnp.mean(e, axis=-1, keepdims=True) - n * jnp.mean(e * n, axis=-1, keepdims=True))


def colsum(x):
    return jnp.sum(x.astype(F32), axis=0, keepdims=True)


def take(x, index, axis):
    return lax.dynamic_index_in_dim(x, index, axis, keepdims=False)


GAIN1, SHIFT1, BQ, BV, BO, GAIN2, SHIFT2, BDOWN = range(8)


def windows():
    out = []
    for h in range(GROUP):
        first, last = h * HEAD_DIM, (h + 1) * HEAD_DIM
        lo, hi = first // 128 * 128, -(-last // 128) * 128
        out.append((lo, hi, first - lo, last - lo))
    return out


def head_lanes(shape, first, last):
    lane = lax.broadcasted_iota(jnp.int32, shape, 1)
    return (lane >= first) & (lane < last)


def turn(x):
    return jnp.transpose(x.astype(F32)).astype(BF16)


def split_rows(x, block, c, keep, send, at=0):
    for i in range(x.shape[0] // (2 * block)):
        even, odd = x[2 * i * block : (2 * i + 1) * block, :], x[(2 * i + 1) * block : (2 * i + 2) * block, :]
        rows = pl.ds(at + i * block, block)
        keep[rows, :] = jnp.where(c == 0, even, odd)
        send[rows, :] = jnp.where(c == 0, odd, even)


def join(refs, rows):
    return jnp.concatenate([r[:rows, :] for r in refs], axis=0)


def column_of(row):
    n = row.shape[1]
    eye = lax.broadcasted_iota(jnp.int32, (n, n), 0) == lax.broadcasted_iota(jnp.int32, (n, n), 1)
    return jnp.sum(jnp.where(eye, row, 0.0), axis=1, keepdims=True)


def attend_kernel(rows, nb, block, core, *refs):
    slots = refs[:nb]
    c = core[0]
    vec, wq, wk, wv, wo = refs[nb : nb + 5]
    keep_o, send_o, q_o, k_o, v_o, mid_o, two_o, mask_o, att_o, kt = refs[nb + 5 :]
    tokens = nb * rows
    half = q_o.shape[1] // 2
    row = jnp.zeros((1, tokens), F32)
    for s in range(nb):
        row = row + slots[s][rows : rows + 8, :tokens].astype(F32)[s : s + 1, :]
    mask_o[...] = jnp.broadcast_to(row, mask_o.shape)
    x = join(slots, rows).astype(F32)
    n1, _ = norm_stats(x)
    normed = (n1 * vec[GAIN1 : GAIN1 + 1, :] + vec[SHIFT1 : SHIFT1 + 1, :]).astype(BF16)
    split_rows(turn(normed), block, c, keep_o, send_o)
    q_o[...] = (dot_nn(normed, wq[...]) + vec[BQ : BQ + 1, :]).astype(BF16)
    k = dot_nn(normed, wk[...]).astype(BF16)
    k_o[...] = k
    kt[...] = turn(k)
    v_o[...] = (dot_nn(normed, wv[...]) + vec[BV : BV + 1, :]).astype(BF16)
    keep = row > 0.5

    def group(g, carry):
        base = pl.multiple_of(g * GROUP_LANES, 128)
        blocks = [jnp.zeros((tokens, 128), F32) for _ in range(GROUP_LANES // 128)]
        for lo, hi, first, last in windows():
            wide = hi - lo
            here = head_lanes((tokens, wide), first, last)
            at = pl.ds(base + lo, wide)
            zero = jnp.zeros((tokens, wide), BF16)
            qm = jnp.where(here, q_o[:, at], zero)
            s = dot_nn(qm, kt[at, :]) * SCALE
            s = jnp.where(keep, s, -1e30)
            e = jnp.exp(s - jnp.max(s, axis=-1, keepdims=True))
            p = (e * (1.0 / jnp.sum(e, axis=-1, keepdims=True))).astype(BF16)
            o = dot_nn(p, jnp.where(here, v_o[:, at], zero))
            for j in range(wide // 128):
                blocks[lo // 128 + j] = blocks[lo // 128 + j] + o[:, j * 128 : (j + 1) * 128]
        att_o[:, pl.ds(base, GROUP_LANES)] = jnp.concatenate(blocks, axis=1).astype(BF16)
        return carry

    lax.fori_loop(0, HEADS // GROUP, group, 0)
    split_rows(turn(att_o[...]), block, c, keep_o, send_o, half)
    middle = x + (dot_nn(att_o[...], wo[...]) + vec[BO : BO + 1, :])
    mid_o[...] = middle
    n2, _ = norm_stats(middle)
    two = (n2 * vec[GAIN2 : GAIN2 + 1, :] + vec[SHIFT2 : SHIFT2 + 1, :]).astype(BF16)
    two_o[...] = two
    split_rows(turn(two), block, c, keep_o, send_o, 2 * half)


def up_kernel(rows, nb, steps, block, core, *refs):
    two, middle, mask, vec, w_up, b_up, w_down = refs[:7]
    cots = refs[7 : 7 + nb]
    act_keep, act_send, right_o, bsum = refs[7 + nb : 11 + nb]
    out_o, acc = refs[11 + nb :]
    j = pl.program_id(0)
    width = acc.shape[1]

    @pl.when(j == 0)
    def _():
        col = column_of(mask[0:1, :])
        right_o[:, :width] = (join(cots, rows).astype(F32) * col).astype(BF16)

    hidden = dot_nn(two[...], w_up[...]) + b_up[0:1, :]
    cdf = 0.5 * (1.0 + lax.erf(hidden * 0.7071067811865476))
    pdf = jnp.exp(-0.5 * hidden * hidden) * 0.3989422804014327
    act = (hidden * cdf).astype(BF16)
    split_rows(turn(act), block, core[0], act_keep, act_send)
    part = dot_nn(act, w_down[...])
    acc[...] = jnp.where(j == 0, part, acc[...] + part)
    gh = (dot_nt(right_o[:, :width], w_down[...]) * (cdf + hidden * pdf)).astype(BF16)
    right_o[:, pl.ds(pl.multiple_of(width + j * gh.shape[1], 128), gh.shape[1])] = gh
    bsum[...] = jnp.broadcast_to(colsum(gh), bsum.shape)

    @pl.when(j == steps - 1)
    def _():
        col = column_of(mask[0:1, :])
        out_o[...] = (col * (middle[...] + (acc[...] + vec[BDOWN : BDOWN + 1, :]))).astype(BF16)


def down_kernel(rows, nb, steps, *refs):
    gd, gh, w_up, middle, mask, vec = refs[:6]
    cots = refs[6 : 6 + nb]
    gm_o, gb_o, sums, acc = refs[6 + nb :]
    j = pl.program_id(0)
    part = dot_nt(gh[...], w_up[...])
    acc[...] = jnp.where(j == 0, part, acc[...] + part)

    @pl.when(j == steps - 1)
    def _():
        grad = acc[...]
        n2, r2 = norm_stats(middle[...])
        col = column_of(mask[0:1, :])
        result = join(cots, rows).astype(F32) * col
        gm = result + norm_back(grad, n2, r2, vec[GAIN2 : GAIN2 + 1, :])
        gm_o[...] = gm
        gb = gm.astype(BF16)
        gb_o[...] = gb
        sums[0:1, :] = colsum(grad * n2)
        sums[1:2, :] = colsum(grad)
        sums[2:3, :] = colsum(gb)
        sums[3:4, :] = colsum(gd[...])
        sums[4:8, :] = jnp.zeros((4, sums.shape[1]), F32)


def attend_back_kernel(gb, q, k, v, mask, wo, right_o, sums, gq_o, ga, qt, kt, vt, gat, gkt, gvt):
    tokens, width = gb.shape
    g_att = dot_nt(gb[...], wo[...]).astype(BF16)
    ga[...] = g_att
    gat[...] = turn(g_att)
    qt[...] = turn(q[...])
    kt[...] = turn(k[...])
    vt[...] = turn(v[...])
    keep = mask[0:1, :] > 0.5

    def group(g, carry):
        base = pl.multiple_of(g * GROUP_LANES, 128)
        blocks = [jnp.zeros((tokens, 128), F32) for _ in range(GROUP_LANES // 128)]
        for h, (lo, hi, first, last) in enumerate(windows()):
            wide = hi - lo
            here = head_lanes((tokens, wide), first, last)
            at = pl.ds(base + lo, wide)
            own = pl.ds(pl.multiple_of(base + h * HEAD_DIM, 16), HEAD_DIM)
            zero = jnp.zeros((tokens, wide), BF16)
            s = dot_nn(jnp.where(here, q[:, at], zero), kt[at, :]) * SCALE
            s = jnp.where(keep, s, -1e30)
            e = jnp.exp(s - jnp.max(s, axis=-1, keepdims=True))
            p = e * (1.0 / jnp.sum(e, axis=-1, keepdims=True))
            dp = dot_nn(jnp.where(here, ga[:, at], zero), vt[at, :])
            gvt[own, :] = dot_nn(gat[own, :], p.astype(BF16))
            ds = (p * (dp - jnp.sum(p * dp, axis=-1, keepdims=True))).astype(BF16)
            gkt[own, :] = dot_nn(qt[own, :], ds)
            o = dot_nn(ds, jnp.where(here, k[:, at], zero))
            for j in range(wide // 128):
                blocks[lo // 128 + j] = blocks[lo // 128 + j] + o[:, j * 128 : (j + 1) * 128]
        gq_o[:, pl.ds(base, GROUP_LANES)] = (jnp.concatenate(blocks, axis=1) * SCALE).astype(BF16)
        return carry

    lax.fori_loop(0, HEADS // GROUP, group, 0)
    gq = gq_o[...]
    gk = (jnp.transpose(gkt[...]) * SCALE).astype(BF16)
    gv = jnp.transpose(gvt[...]).astype(BF16)
    for i, t in enumerate((gq, gk, gv)):
        right_o[:, i * width : (i + 1) * width] = t
    sums[0:1, :] = colsum(gq)
    sums[1:2, :] = colsum(gv)
    sums[2:8, :] = jnp.zeros((6, width), F32)


def by_band(rows, nb, band, x, own, near, far):
    for bits, out, at in ((0, own, 0), (1, near, 0), (3, near, rows), (2, far, 0)):
        slot = lax.rem(band[0] - jnp.bitwise_xor(band[0], bits) + nb, nb)
        out[at : at + rows, :] = x[pl.ds(pl.multiple_of(slot * rows, 16), rows), :]


def input_back_kernel(rows, nb, block, core, band, *refs):
    slots = refs[:nb]
    right, wq, wk, wv, gm, vec, down_sums, attend_sums, up_cols = refs[nb : nb + 9]
    own_o, near_o, far_o, keep_o, send_o, held = refs[nb + 9 :]
    width = gm.shape[1]
    grad = dot_nt(right[:, :width], wq[...])
    grad = grad + dot_nt(right[:, width : 2 * width], wk[...])
    grad = grad + dot_nt(right[:, 2 * width :], wv[...])
    n1, r1 = norm_stats(join(slots, rows).astype(F32))
    gx = (gm[...] + norm_back(grad, n1, r1, vec[GAIN1 : GAIN1 + 1, :])).astype(BF16)
    held[...] = gx
    by_band(rows, nb, band, held, own_o, near_o, far_o)
    table = jnp.concatenate(
        [
            down_sums[...], attend_sums[...], colsum(grad * n1), colsum(grad),
            jnp.zeros((COLS - 18, width), F32),
        ],
        axis=0,
    )
    split_rows(jnp.transpose(table) + up_cols[...], block, core[0], keep_o, send_o)


def spread_kernel(rows, nb, band, crop_rows, crop_cols, x, keep_mask, *outs):
    width = x.shape[2]
    position = band[0] * rows + lax.broadcasted_iota(jnp.int32, (1, rows), 1)
    slot = lax.broadcasted_iota(jnp.int32, (8, width), 0)
    lane = lax.broadcasted_iota(jnp.int32, (8, width), 1) // rows
    for s in range(nb):
        image = lax.rem(band[0] + s, nb)
        outs[s][:rows, :] = x[image]
        inside = (
            (keep_mask[pl.ds(image, 1), :] > 0)
            & (position // SIDE < crop_rows[image])
            & (position % SIDE < crop_cols[image])
        )
        flags = jnp.concatenate([jnp.where(inside, 1.0, 0.0)] * (width // rows), axis=1)
        outs[s][rows:, :] = jnp.where((slot == s) & (lane == s), flags, 0.0).astype(BF16)


def gather_kernel(band, *refs):
    output, grad = refs[6:]
    rows = output.shape[1]
    for out, (own, near, far) in ((output, refs[:3]), (grad, refs[3:6])):
        for bits, ref, at in ((0, own, 0), (1, near, 0), (2, far, 0), (3, far, rows)):
            out[jnp.bitwise_xor(band[0], bits)] = ref[at : at + rows, :].astype(out.dtype)


def weight_kernel(groups, extra, quarters, *refs):
    t = pl.program_id(0)
    parts, at = [], 0
    for widths in groups:
        left, left_got = refs[at : at + 2]
        at += 2
        for _ in widths:
            right, right_got = refs[at : at + 2]
            at += 2
            parts.append((dot_nn(left[...], right[...]) + dot_nn(left_got[...], right_got[...])).astype(BF16))
    if extra:
        parts.append((refs[at][...] + refs[at + 1][...]).astype(BF16))
        at += 2
    send, keep = refs[at:]
    g = parts[0] if len(parts) == 1 else jnp.concatenate(parts, axis=1)

    @pl.when(t < 2)
    def _():
        send[0] = g

    @pl.when(t >= 2)
    def _():
        keep[0] = g


def second_kernel(keep, got, out):
    out[...] = (keep[0].astype(F32) + got[0].astype(F32)).astype(BF16)


def third_kernel(size, band, keep, got, more, keep_o, send_o, held):
    held[...] = keep[0].astype(F32) + got[0].astype(F32) + more[...].astype(F32)
    for i in range(2):
        near = jnp.bitwise_xor(band[0], 2 * i)
        far = jnp.bitwise_xor(band[0], 2 * i + 1)
        keep_o[i] = held[pl.ds(pl.multiple_of(near * size, 8), size), :]
        send_o[i] = held[pl.ds(pl.multiple_of(far * size, 8), size), :].astype(BF16)


def last_kernel(widths, vectors, keep, got, more, *outs):
    at = 0
    for w, out in zip(widths, outs):
        cols = pl.ds(at, w)
        out[...] = keep[0, :, cols] + got[0, :, cols].astype(F32) + more[:, cols].astype(F32)
        at += w
    if vectors:
        cols = pl.ds(at, COLS)
        table = jnp.transpose(keep[0, :, cols] + got[0, :, cols].astype(F32) + more[:, cols].astype(F32))
        for (first, n), out in zip(vectors, outs[len(widths) :]):
            out[...] = jnp.concatenate([table[first + i : first + i + 1, :] for i in range(n)], axis=1)


COLS = 128
LIMIT = pltpu.CompilerParams(vmem_limit_bytes=20 * 1024 * 1024)
USED = (16, 17, 8, 9, 2, 0, 1, 3)


VM = pl.BlockSpec(memory_space=pltpu.VMEM)
SM = pl.BlockSpec(memory_space=pltpu.SMEM)


def shape(*dims, dtype=BF16):
    return jax.ShapeDtypeStruct(dims, dtype)


def cost(us):
    return pl.CostEstimate(flops=int(us * 2500000000), bytes_accessed=int(us * 10000000), transcendentals=0)


def after(x, *others):
    return lax.optimization_barrier((x, others))[0]


def scalar(x):
    return x.astype(jnp.int32).reshape(1)


class Links:
    def __init__(self, n_img, n_band):
        self.n_img, self.nb = n_img, n_band
        self.hi = n_img // 8
        i = lax.axis_index("img")
        self.c = i & 1
        self.p = (i >> 1) & 1
        self.q = (i >> 2) & 1
        self.h = i >> 3
        self.b = lax.axis_index("band")

    def flip(self, x, bit):
        return lax.ppermute(x, "img", [(k, k ^ bit) for k in range(self.n_img)])

    def flip_by_core(self, x, even, odd):
        return lax.ppermute(x, "img", [(k, k ^ (odd if k & 1 else even)) for k in range(self.n_img)])

    def flip_band(self, x, bit):
        return lax.ppermute(x, "band", [(k, k ^ bit) for k in range(self.nb)])

    def band_shift(self, x, s):
        return lax.ppermute(x, "band", [(k, (k + s) % self.nb) for k in range(self.nb)])

    def hi_shift(self, x, s):
        n = self.n_img
        return lax.ppermute(x, "img", [(k, (k + 8 * s) % n) for k in range(n)])

    def sum_hi(self, x):
        x = x.reshape(self.hi, x.shape[0] // self.hi, *x.shape[1:])
        total = take(x, self.h, 0)
        for s in range(1, self.hi):
            total = total + self.hi_shift(take(x, (self.h + s) % self.hi, 0).astype(BF16), s).astype(F32)
        return total

    def by_quarter(self, x):
        if self.hi == 1:
            return x
        return x.reshape(self.hi, 4, -1, x.shape[1]).swapaxes(0, 1).reshape(x.shape)

    def reclass(self, first, second, block):
        x = jnp.concatenate([first, second], axis=0)
        x = x.reshape(-1, 2, block, x.shape[1])
        own, other = take(x, self.c, 1), take(x, 1 - self.c, 1)
        return own.reshape(-1, x.shape[3]), other.reshape(-1, x.shape[3])


class Unit:
    def __init__(self, links, rows, groups, extra=()):
        self.links, self.vectors = links, []
        args, specs, widths = [], [], []
        tokens = groups[0][0].shape[1]
        self.block = block = rows // 4
        for left, left_got, left_at, rights in groups:
            if links.hi > 1:
                left, left_got = (x[left_at * rows : (left_at + 1) * rows, :] for x in (left, left_got))
                left_at = 0
            args += [links.by_quarter(left), links.by_quarter(left_got)]
            specs += [pl.BlockSpec((block, tokens), lambda t, s, i=4 * left_at: (s[t] + i, 0))] * 2
            widths.append([w for w, _, _, _, _ in rights])
            for w, own, own_at, got, got_at in rights:
                args += [own, got]
                specs.append(pl.BlockSpec((tokens, w), lambda t, s, i=own_at: (0, i)))
                specs.append(pl.BlockSpec((tokens, w), lambda t, s, i=got_at: (0, i)))
        for x in extra:
            args.append(links.by_quarter(x))
            specs.append(pl.BlockSpec((block, COLS), lambda t, s: (s[t], 0)))
        self.extra = len(extra) > 0
        self.widths = [w for ws in widths for w in ws] + [COLS] * self.extra
        self.cols = cols = sum(self.widths)
        p, q = links.p, links.q
        even = links.c == 0
        at = lambda a, b: a * 2 + b
        quarters = jnp.stack(
            [
                jnp.where(even, at(q, 1 - p), at(1 - q, p)), at(1 - q, 1 - p),
                jnp.where(even, at(1 - q, p), at(q, 1 - p)), at(q, p),
            ]
        ).astype(jnp.int32)
        one = lambda x: jnp.asarray(x).astype(jnp.int32)
        self.send, self.keep = pl.pallas_call(
            functools.partial(weight_kernel, widths, self.extra),
            grid_spec=pltpu.PrefetchScalarGridSpec(
                num_scalar_prefetch=1,
                grid=(4,),
                in_specs=specs,
                out_specs=[
                    pl.BlockSpec((1, block, cols), lambda t, s: (one(t > 0), 0, 0)),
                    pl.BlockSpec((1, block, cols), lambda t, s: (one(t < 3), 0, 0)),
                ],
            ),
            out_shape=[shape(2, block, cols)] * 2,
            cost_estimate=cost(0.1 if extra else 6),
            compiler_params=LIMIT,
            name="weight_grad",
        )(quarters, *args)
        self.got = links.flip_by_core(self.send, 2, 4)

    def pick(self, i):
        return pl.BlockSpec((1, self.block, self.cols), lambda _: (i, 0, 0))

    def whole(self, *dims):
        return pl.BlockSpec(dims, lambda _: (0,) * len(dims))

    def second(self, *deps):
        dims = (self.block, self.cols)
        sent = pl.pallas_call(
            second_kernel,
            grid=(1,),
            in_specs=[self.pick(1)] * 2,
            out_specs=self.whole(*dims),
            out_shape=shape(*dims),
            cost_estimate=cost(2),
            compiler_params=LIMIT,
            name="second",
        )(after(self.keep, *deps), self.got)
        self.more = self.links.flip_by_core(sent, 4, 2)
        return sent

    def third(self, *deps):
        links, nb, cols = self.links, self.links.nb, self.cols
        self.size = size = self.block // (links.hi * nb)
        keep = after(self.keep, *deps)
        if links.hi > 1 or size % 8:
            held = links.sum_hi(keep[0].astype(F32) + self.got[0].astype(F32) + self.more.astype(F32))
            held = held.reshape(nb, size, cols)
            piece = lambda bits: take(held, links.b ^ bits, 0)
            self.near = jnp.stack([piece(0), piece(2)])
            sent = jnp.stack([piece(1), piece(3)]).astype(BF16)
        else:
            self.near, sent = pl.pallas_call(
                functools.partial(third_kernel, size),
                grid=(1,),
                in_specs=[SM, self.pick(0), self.pick(0), self.whole(self.block, cols)],
                out_specs=[self.whole(2, size, cols)] * 2,
                out_shape=[shape(2, size, cols, dtype=F32), shape(2, size, cols)],
                scratch_shapes=[pltpu.VMEM((self.block, cols), F32)],
                cost_estimate=cost(3),
                compiler_params=LIMIT,
                name="third",
            )(scalar(links.b), keep, self.got, self.more)
        self.near_got = links.flip_band(sent, 1)
        return sent

    def fourth(self, *deps):
        dims = (self.size, self.cols)
        pick = pl.BlockSpec((1,) + dims, lambda _: (1, 0, 0))
        sent = pl.pallas_call(
            second_kernel,
            grid=(1,),
            in_specs=[pick] * 2,
            out_specs=self.whole(*dims),
            out_shape=shape(*dims),
            cost_estimate=cost(2),
            compiler_params=LIMIT,
            name="fourth",
        )(after(self.near, *deps), self.near_got)
        self.far_got = self.links.flip_band(sent, 2)
        return sent

    def last(self, *deps):
        dims = (self.size, self.cols)
        pick = pl.BlockSpec((1,) + dims, lambda _: (0, 0, 0))
        vectors = self.vectors
        outs = [(self.size, w) for w in self.widths] + [(1, n * self.size) for _, n in vectors]
        return pl.pallas_call(
            functools.partial(last_kernel, self.widths, vectors),
            grid=(1,),
            in_specs=[pick, pick, self.whole(*dims)],
            out_specs=[self.whole(*d) for d in outs],
            out_shape=[shape(*d, dtype=F32) for d in outs],
            cost_estimate=cost(2),
            compiler_params=LIMIT,
            name="last",
        )(after(self.near, *deps), self.near_got, self.far_got)


def per_device(
    inputs, keep_mask, crop_rows, crop_cols, gain_one, shift_one, w_query, b_query, w_key, w_value,
    b_value, w_out, b_out, gain_two, shift_two, w_up, b_up, w_down, b_down, cotangent, *, n_img, nb,
):
    images, rows, width = inputs.shape
    hidden_width = w_up.shape[1]
    assert images == nb and nb == 4
    tokens = nb * rows
    links = Links(n_img, nb)
    core, band = scalar(links.c), scalar(links.b)
    f = lambda v: v.astype(F32)

    blocks = pl.pallas_call(
        functools.partial(spread_kernel, rows, nb),
        in_specs=[SM] * 3 + [VM] * 2,
        out_specs=[VM] * nb,
        out_shape=[shape(rows + 8, width)] * nb,
        cost_estimate=cost(2),
        name="spread",
    )(band, crop_rows, crop_cols, inputs, keep_mask)
    slots = [blocks[0]] + [links.band_shift(blocks[s], s) for s in range(1, nb)]
    given = after(cotangent, *blocks)
    cots = [take(given, links.b, 0)]
    for s in range(1, nb):
        cots.append(links.band_shift(take(given, (links.b + s) % nb, 0), s))
    vec = jnp.stack([f(t) for t in (gain_one, shift_one, b_query, b_value, b_out, gain_two, shift_two, b_down)])
    b_up_row = f(b_up)[None, :]

    block = width // (links.hi * 8)
    aligned = block % 16 == 0
    up_block = hidden_width // (links.hi * 8)
    half = width // 2
    full = shape(tokens, width)
    left_keep, left_send, q, k, v, middle, two, mask = pl.pallas_call(
        functools.partial(attend_kernel, rows, nb, block if aligned else half),
        in_specs=[SM] + [VM] * (nb + 5),
        out_specs=[VM] * 8,
        out_shape=[shape(3 * half, tokens)] * 2 + [full] * 3
        + [shape(tokens, width, dtype=F32), full, shape(8, tokens, dtype=F32)],
        scratch_shapes=[pltpu.VMEM((tokens, width), BF16), pltpu.VMEM((width, tokens), BF16)],
        cost_estimate=cost(9),
        name="attend",
    )(core if aligned else jnp.zeros_like(core), *slots, vec, w_query, w_key, w_value, w_out)
    third_of = lambda x, i: x[i * half : (i + 1) * half, :]
    if not aligned:
        pairs = [links.reclass(third_of(left_keep, i), third_of(left_send, i), block) for i in range(3)]
        left_keep, left_send = (jnp.concatenate(x, axis=0) for x in zip(*pairs))
    left_got = links.flip(left_send, 1)

    steps = 4
    wide = hidden_width // steps
    fixed = lambda *dims: pl.BlockSpec(dims, lambda j, *_: (0,) * len(dims))
    tall = lambda *dims: pl.BlockSpec(dims, lambda j, *_: (0, j))
    up = pl.pallas_call(
        functools.partial(up_kernel, rows, nb, steps, up_block),
        grid_spec=pltpu.PrefetchScalarGridSpec(
            num_scalar_prefetch=1,
            grid=(steps,),
            in_specs=[
                fixed(tokens, width), fixed(tokens, width), fixed(8, tokens), fixed(8, width),
                tall(width, wide), tall(1, wide),
                pl.BlockSpec((wide, width), lambda j, c: (j, 0)),
            ] + [fixed(rows, width)] * nb,
            out_specs=[pl.BlockSpec((wide // 2, tokens), lambda j, c: (j, 0))] * 2
            + [fixed(tokens, width + hidden_width), tall(8, wide), fixed(tokens, width)],
            scratch_shapes=[pltpu.VMEM((tokens, width), F32)],
        ),
        out_shape=[shape(hidden_width // 2, tokens)] * 2
        + [shape(tokens, width + hidden_width), shape(8, hidden_width, dtype=F32), full],
        cost_estimate=cost(10),
        name="up",
    )(core, two, middle, mask, vec, w_up, b_up_row, w_down, *cots)
    act_keep, act_send, right, up_sums, result = up
    act_got = links.flip(act_send, 1)
    right_got = links.flip(right, 1)

    grad_middle, grad_branch, down_sums = pl.pallas_call(
        functools.partial(down_kernel, rows, nb, steps),
        grid=(steps,),
        in_specs=[
            fixed(tokens, width), pl.BlockSpec((tokens, wide), lambda j: (0, j + width // wide)), tall(width, wide),
            fixed(tokens, width), fixed(8, tokens), fixed(8, width),
        ] + [fixed(rows, width)] * nb,
        out_specs=[fixed(tokens, width), fixed(tokens, width), fixed(8, width)],
        out_shape=[shape(tokens, width, dtype=F32), full, shape(8, width, dtype=F32)],
        scratch_shapes=[pltpu.VMEM((tokens, width), F32)],
        cost_estimate=cost(7),
        name="down",
    )(right, right, w_up, after(middle, left_got), mask, vec, *cots)
    branch_got = links.flip(grad_branch, 1)

    unit_down = Unit(
        links, hidden_width // 2,
        [(after(act_keep, grad_branch), act_got, 0, [(width, right, 0, right_got, 0)])],
    )
    unit_up = Unit(
        links, half,
        [
            (
                after(left_keep, unit_down.send), left_got, 2,
                [(width, right, 1 + i, right_got, 1 + i) for i in range(hidden_width // width)],
            ),
            (left_keep, left_got, 1, [(width, grad_branch, 0, branch_got, 0)]),
        ],
    )
    low = lambda: pltpu.VMEM((width, tokens), BF16)
    back_right, attend_sums = pl.pallas_call(
        attend_back_kernel,
        in_specs=[VM] * 6,
        out_specs=[VM] * 2,
        out_shape=[shape(tokens, 3 * width), shape(8, width, dtype=F32)],
        scratch_shapes=[
            pltpu.VMEM((tokens, width), BF16), pltpu.VMEM((tokens, width), BF16), low(), low(), low(), low(),
            pltpu.VMEM((width, tokens), F32), pltpu.VMEM((width, tokens), F32),
        ],
        cost_estimate=cost(11),
        compiler_params=LIMIT,
        name="attend_back",
    )(after(grad_branch, unit_up.send), q, k, v, mask, w_out)
    back_got = links.flip(back_right, 1)

    results = pl.pallas_call(
        functools.partial(by_band, rows, nb),
        in_specs=[SM, VM],
        out_specs=[VM] * 3,
        out_shape=[shape(rows, width), shape(2 * rows, width), shape(rows, width)],
        cost_estimate=cost(1),
        compiler_params=LIMIT,
        name="by_band",
    )(band, after(result, unit_up.send))
    result_near = links.flip_band(results[1], 1)
    mark = unit_down.second(back_right)
    per_row = hidden_width // width
    up_cols = up_sums[0].reshape(n_img * nb, per_row, -1).swapaxes(1, 2).reshape(width, per_row)
    up_cols = jnp.pad(up_cols, ((0, 0), (18, COLS - 18 - per_row)))
    back = pl.pallas_call(
        functools.partial(input_back_kernel, rows, nb, block if aligned else half),
        in_specs=[SM] * 2 + [VM] * (nb + 9),
        out_specs=[VM] * 5,
        out_shape=[shape(rows, width), shape(2 * rows, width), shape(rows, width)]
        + [shape(half, COLS, dtype=F32)] * 2,
        scratch_shapes=[pltpu.VMEM((tokens, width), BF16)],
        cost_estimate=cost(5),
        compiler_params=LIMIT,
        name="input_back",
    )(
        core if aligned else jnp.zeros_like(core), band,
        *slots, after(back_right, mark), w_query, w_key, w_value, grad_middle, vec, down_sums, attend_sums, up_cols,
    )
    blocks, table = back[:3], back[3:]
    near_got = links.flip_band(blocks[1], 1)
    if not aligned:
        table = links.reclass(*table, block)
    table_got = links.flip(table[1], 1)

    unit_qkv = Unit(
        links, half,
        [(after(left_keep, blocks[0]), left_got, 0, [(width, back_right, i, back_got, i) for i in range(3)])],
        (table[0], table_got),
    )
    result_far = links.flip_band(jnp.concatenate([after(results[2], blocks[0]), result_near[rows:, :]]), 2)
    far_got = links.flip_band(jnp.concatenate([after(blocks[2], unit_qkv.send), near_got[rows:, :]]), 2)
    mark = unit_up.second(unit_qkv.send)
    mark = unit_down.third(mark)
    mark = unit_qkv.second(mark)
    mark = unit_up.third(mark)
    mark = unit_down.fourth(mark)
    mark = unit_qkv.third(mark)
    mark = unit_up.fourth(mark)
    mark = unit_qkv.fourth(mark)
    (g_w_down,) = unit_down.last(mark)
    output, grad_inputs = pl.pallas_call(
        gather_kernel,
        in_specs=[SM] + [VM] * 6,
        out_specs=[VM] * 2,
        out_shape=[shape(nb, rows, width), shape(nb, rows, width, dtype=F32)],
        cost_estimate=cost(2),
        compiler_params=LIMIT,
        name="gather",
    )(after(band, g_w_down), results[0], result_near, result_far, blocks[0], near_got, far_got)
    mark = output
    unit_up.widths = [hidden_width, width]
    g_w_up, g_w_out = unit_up.last(mark)
    if unit_qkv.size % 8 == 0:
        unit_qkv.widths = [width] * 3
        unit_qkv.vectors = [(i, 1) for i in USED] + [(18, per_row)]
        g_w_query, g_w_key, g_w_value, *rest = unit_qkv.last(g_w_up)
        sums = {i: x[0] for i, x in zip(USED + (18,), rest)}
    else:
        g_w_query, g_w_key, g_w_value, cols = unit_qkv.last(g_w_up)
        sums = [cols[:, i] for i in range(18)] + [cols[:, 18 : 18 + per_row].swapaxes(0, 1).reshape(-1)]
    return (
        output,
        grad_inputs,
        sums[16],
        sums[17],
        g_w_query,
        sums[8],
        g_w_key,
        g_w_value,
        sums[9],
        g_w_out,
        sums[2],
        sums[0],
        sums[1],
        g_w_up,
        sums[18],
        g_w_down,
        sums[3],
    )


def solution(mesh):
    n_img, nb = mesh.shape["img"], mesh.shape["band"]

    def body(*args):
        return per_device(*args, n_img=n_img, nb=nb)

    both = P(("img", "band"))
    rows = P(("img", "band"), None)
    token = P("img", "band", None)
    return jax.shard_map(
        body,
        mesh=mesh,
        in_specs=(token, P("img", "band"), P("img"), P("img")) + (P(),) * 15 + (token,),
        out_specs=(
            token, token, both, both, rows, both, rows, rows, both, rows, both, both, both, rows, both,
            rows, both,
        ),
        check_vma=False,
    )
```

```python
import functools

import jax
import jax.numpy as jnp
from jax import lax
from jax.experimental import pallas as pl
from jax.experimental.pallas import tpu as pltpu
from jax.sharding import PartitionSpec as P

HEADS = 16
HEAD_DIM = 48
SIDE = 16
EPS = 1e-05
F32 = jnp.float32
BF16 = jnp.bfloat16
GROUP = 8
GROUP_LANES = GROUP * HEAD_DIM
SCALE = HEAD_DIM ** (-0.5)


def dot_nn(a, b):
    return lax.dot_general(a, b, (((1,), (0,)), ((), ())), preferred_element_type=F32)


def dot_nt(a, b):
    return lax.dot_general(a, b, (((1,), (1,)), ((), ())), preferred_element_type=F32)


def dot_tn(a, b):
    return lax.dot_general(a, b, (((0,), (0,)), ((), ())), preferred_element_type=F32)


def norm_stats(x):
    mean = jnp.mean(x, axis=-1, keepdims=True)
    centred = x - mean
    var = jnp.mean(centred * centred, axis=-1, keepdims=True)
    r = lax.rsqrt(var + EPS)
    return centred * r, r


def norm_back(grad, n, r, gain):
    e = grad * gain
    return r * (e - jnp.mean(e, axis=-1, keepdims=True) - n * jnp.mean(e * n, axis=-1, keepdims=True))


def colsum(x):
    return jnp.sum(x.astype(F32), axis=0, keepdims=True)


def take(x, index, axis):
    return lax.dynamic_index_in_dim(x, index, axis, keepdims=False)


GAIN1, SHIFT1, BQ, BV, BO, GAIN2, SHIFT2, BDOWN = range(8)


def windows():
    out = []
    for h in range(GROUP):
        first, last = h * HEAD_DIM, (h + 1) * HEAD_DIM
        lo, hi = first // 128 * 128, -(-last // 128) * 128
        out.append((lo, hi, first - lo, last - lo))
    return out


def head_lanes(shape, first, last):
    lane = lax.broadcasted_iota(jnp.int32, shape, 1)
    return (lane >= first) & (lane < last)


def turn(x):
    return jnp.transpose(x.astype(F32)).astype(BF16)


def split_rows(x, block, c, keep, send, at=0):
    for i in range(x.shape[0] // (2 * block)):
        even, odd = x[2 * i * block : (2 * i + 1) * block, :], x[(2 * i + 1) * block : (2 * i + 2) * block, :]
        rows = pl.ds(at + i * block, block)
        keep[rows, :] = jnp.where(c == 0, even, odd)
        send[rows, :] = jnp.where(c == 0, odd, even)


def join(refs, rows):
    return jnp.concatenate([r[:rows, :] for r in refs], axis=0)


def column_of(row):
    n = row.shape[1]
    eye = lax.broadcasted_iota(jnp.int32, (n, n), 0) == lax.broadcasted_iota(jnp.int32, (n, n), 1)
    return jnp.sum(jnp.where(eye, row, 0.0), axis=1, keepdims=True)


def attend_kernel(rows, nb, block, core, *refs):
    slots = refs[:nb]
    c = core[0]
    vec, wq, wk, wv, wo = refs[nb : nb + 5]
    keep_o, send_o, q_o, k_o, v_o, mid_o, two_o, mask_o, att_o, kt = refs[nb + 5 :]
    tokens = nb * rows
    half = q_o.shape[1] // 2
    row = jnp.zeros((1, tokens), F32)
    for s in range(nb):
        row = row + slots[s][rows : rows + 8, :tokens].astype(F32)[s : s + 1, :]
    mask_o[...] = jnp.broadcast_to(row, mask_o.shape)
    x = join(slots, rows).astype(F32)
    n1, _ = norm_stats(x)
    normed = (n1 * vec[GAIN1 : GAIN1 + 1, :] + vec[SHIFT1 : SHIFT1 + 1, :]).astype(BF16)
    split_rows(turn(normed), block, c, keep_o, send_o)
    q_o[...] = (dot_nn(normed, wq[...]) + vec[BQ : BQ + 1, :]).astype(BF16)
    k = dot_nn(normed, wk[...]).astype(BF16)
    k_o[...] = k
    kt[...] = turn(k)
    v_o[...] = (dot_nn(normed, wv[...]) + vec[BV : BV + 1, :]).astype(BF16)
    keep = row > 0.5

    def group(g, carry):
        base = pl.multiple_of(g * GROUP_LANES, 128)
        blocks = [jnp.zeros((tokens, 128), F32) for _ in range(GROUP_LANES // 128)]
        for lo, hi, first, last in windows():
            wide = hi - lo
            here = head_lanes((tokens, wide), first, last)
            at = pl.ds(base + lo, wide)
            zero = jnp.zeros((tokens, wide), BF16)
            qm = jnp.where(here, q_o[:, at], zero)
            s = dot_nn(qm, kt[at, :]) * SCALE
            s = jnp.where(keep, s, -1e30)
            e = jnp.exp(s - jnp.max(s, axis=-1, keepdims=True))
            p = (e * (1.0 / jnp.sum(e, axis=-1, keepdims=True))).astype(BF16)
            o = dot_nn(p, jnp.where(here, v_o[:, at], zero))
            for j in range(wide // 128):
                blocks[lo // 128 + j] = blocks[lo // 128 + j] + o[:, j * 128 : (j + 1) * 128]
        att_o[:, pl.ds(base, GROUP_LANES)] = jnp.concatenate(blocks, axis=1).astype(BF16)
        return carry

    lax.fori_loop(0, HEADS // GROUP, group, 0)
    split_rows(turn(att_o[...]), block, c, keep_o, send_o, half)
    middle = x + (dot_nn(att_o[...], wo[...]) + vec[BO : BO + 1, :])
    mid_o[...] = middle
    n2, _ = norm_stats(middle)
    two = (n2 * vec[GAIN2 : GAIN2 + 1, :] + vec[SHIFT2 : SHIFT2 + 1, :]).astype(BF16)
    two_o[...] = two
    split_rows(turn(two), block, c, keep_o, send_o, 2 * half)


def up_kernel(rows, nb, steps, block, core, *refs):
    two, middle, mask, vec, w_up, b_up, w_down = refs[:7]
    cots = refs[7 : 7 + nb]
    act_keep, act_send, right_o, bsum = refs[7 + nb : 11 + nb]
    out_o, acc = refs[11 + nb :]
    j = pl.program_id(0)
    width = acc.shape[1]

    @pl.when(j == 0)
    def _():
        col = column_of(mask[0:1, :])
        right_o[:, :width] = (join(cots, rows).astype(F32) * col).astype(BF16)

    hidden = dot_nn(two[...], w_up[...]) + b_up[0:1, :]
    cdf = 0.5 * (1.0 + lax.erf(hidden * 0.7071067811865476))
    pdf = jnp.exp(-0.5 * hidden * hidden) * 0.3989422804014327
    act = (hidden * cdf).astype(BF16)
    split_rows(turn(act), block, core[0], act_keep, act_send)
    part = dot_nn(act, w_down[...])
    acc[...] = jnp.where(j == 0, part, acc[...] + part)
    gh = (dot_nt(right_o[:, :width], w_down[...]) * (cdf + hidden * pdf)).astype(BF16)
    right_o[:, pl.ds(pl.multiple_of(width + j * gh.shape[1], 128), gh.shape[1])] = gh
    bsum[...] = jnp.broadcast_to(colsum(gh), bsum.shape)

    @pl.when(j == steps - 1)
    def _():
        col = column_of(mask[0:1, :])
        out_o[...] = (col * (middle[...] + (acc[...] + vec[BDOWN : BDOWN + 1, :]))).astype(BF16)


def down_kernel(rows, nb, steps, *refs):
    gd, gh, w_up, middle, mask, vec = refs[:6]
    cots = refs[6 : 6 + nb]
    gm_o, gb_o, sums, acc = refs[6 + nb :]
    j = pl.program_id(0)
    part = dot_nt(gh[...], w_up[...])
    acc[...] = jnp.where(j == 0, part, acc[...] + part)

    @pl.when(j == steps - 1)
    def _():
        grad = acc[...]
        n2, r2 = norm_stats(middle[...])
        col = column_of(mask[0:1, :])
        result = join(cots, rows).astype(F32) * col
        gm = result + norm_back(grad, n2, r2, vec[GAIN2 : GAIN2 + 1, :])
        gm_o[...] = gm
        gb = gm.astype(BF16)
        gb_o[...] = gb
        sums[0:1, :] = colsum(grad * n2)
        sums[1:2, :] = colsum(grad)
        sums[2:3, :] = colsum(gb)
        sums[3:4, :] = colsum(gd[...])
        sums[4:8, :] = jnp.zeros((4, sums.shape[1]), F32)


def attend_back_kernel(gb, q, k, v, mask, wo, right_o, sums, gq_o, ga, qt, kt, vt, gat, gkt, gvt):
    tokens, width = gb.shape
    g_att = dot_nt(gb[...], wo[...]).astype(BF16)
    ga[...] = g_att
    gat[...] = turn(g_att)
    qt[...] = turn(q[...])
    kt[...] = turn(k[...])
    vt[...] = turn(v[...])
    keep = mask[0:1, :] > 0.5

    def group(g, carry):
        base = pl.multiple_of(g * GROUP_LANES, 128)
        blocks = [jnp.zeros((tokens, 128), F32) for _ in range(GROUP_LANES // 128)]
        for h, (lo, hi, first, last) in enumerate(windows()):
            wide = hi - lo
            here = head_lanes((tokens, wide), first, last)
            at = pl.ds(base + lo, wide)
            own = pl.ds(pl.multiple_of(base + h * HEAD_DIM, 16), HEAD_DIM)
            zero = jnp.zeros((tokens, wide), BF16)
            s = dot_nn(jnp.where(here, q[:, at], zero), kt[at, :]) * SCALE
            s = jnp.where(keep, s, -1e30)
            e = jnp.exp(s - jnp.max(s, axis=-1, keepdims=True))
            p = e * (1.0 / jnp.sum(e, axis=-1, keepdims=True))
            dp = dot_nn(jnp.where(here, ga[:, at], zero), vt[at, :])
            gvt[own, :] = dot_nn(gat[own, :], p.astype(BF16))
            ds = (p * (dp - jnp.sum(p * dp, axis=-1, keepdims=True))).astype(BF16)
            gkt[own, :] = dot_nn(qt[own, :], ds)
            o = dot_nn(ds, jnp.where(here, k[:, at], zero))
            for j in range(wide // 128):
                blocks[lo // 128 + j] = blocks[lo // 128 + j] + o[:, j * 128 : (j + 1) * 128]
        gq_o[:, pl.ds(base, GROUP_LANES)] = (jnp.concatenate(blocks, axis=1) * SCALE).astype(BF16)
        return carry

    lax.fori_loop(0, HEADS // GROUP, group, 0)
    gq = gq_o[...]
    gk = (jnp.transpose(gkt[...]) * SCALE).astype(BF16)
    gv = jnp.transpose(gvt[...]).astype(BF16)
    for i, t in enumerate((gq, gk, gv)):
        right_o[:, i * width : (i + 1) * width] = t
    sums[0:1, :] = colsum(gq)
    sums[1:2, :] = colsum(gv)
    sums[2:8, :] = jnp.zeros((6, width), F32)


def by_band(rows, nb, band, x, own, near, far):
    for bits, out, at in ((0, own, 0), (1, near, 0), (3, near, rows), (2, far, 0)):
        slot = lax.rem(band[0] - jnp.bitwise_xor(band[0], bits) + nb, nb)
        out[at : at + rows, :] = x[pl.ds(pl.multiple_of(slot * rows, 16), rows), :]


def input_back_kernel(rows, nb, block, core, band, *refs):
    slots = refs[:nb]
    right, wq, wk, wv, gm, vec, down_sums, attend_sums, up_cols = refs[nb : nb + 9]
    own_o, near_o, far_o, keep_o, send_o, held = refs[nb + 9 :]
    width = gm.shape[1]
    grad = dot_nt(right[:, :width], wq[...])
    grad = grad + dot_nt(right[:, width : 2 * width], wk[...])
    grad = grad + dot_nt(right[:, 2 * width :], wv[...])
    n1, r1 = norm_stats(join(slots, rows).astype(F32))
    gx = (gm[...] + norm_back(grad, n1, r1, vec[GAIN1 : GAIN1 + 1, :])).astype(BF16)
    held[...] = gx
    by_band(rows, nb, band, held, own_o, near_o, far_o)
    table = jnp.concatenate(
        [
            down_sums[...], attend_sums[...], colsum(grad * n1), colsum(grad),
            jnp.zeros((COLS - 18, width), F32),
        ],
        axis=0,
    )
    split_rows(jnp.transpose(table) + up_cols[...], block, core[0], keep_o, send_o)


def spread_kernel(rows, nb, band, crop_rows, crop_cols, x, keep_mask, *outs):
    width = x.shape[2]
    position = band[0] * rows + lax.broadcasted_iota(jnp.int32, (1, rows), 1)
    slot = lax.broadcasted_iota(jnp.int32, (8, width), 0)
    lane = lax.broadcasted_iota(jnp.int32, (8, width), 1) // rows
    for s in range(nb):
        image = lax.rem(band[0] + s, nb)
        outs[s][:rows, :] = x[image]
        inside = (
            (keep_mask[pl.ds(image, 1), :] > 0)
            & (position // SIDE < crop_rows[image])
            & (position % SIDE < crop_cols[image])
        )
        flags = jnp.concatenate([jnp.where(inside, 1.0, 0.0)] * (width // rows), axis=1)
        outs[s][rows:, :] = jnp.where((slot == s) & (lane == s), flags, 0.0).astype(BF16)


def gather_kernel(band, *refs):
    output, grad = refs[6:]
    rows = output.shape[1]
    for out, (own, near, far) in ((output, refs[:3]), (grad, refs[3:6])):
        for bits, ref, at in ((0, own, 0), (1, near, 0), (2, far, 0), (3, far, rows)):
            out[jnp.bitwise_xor(band[0], bits)] = ref[at : at + rows, :].astype(out.dtype)


def weight_kernel(groups, extra, quarters, *refs):
    t = pl.program_id(0)
    parts, at = [], 0
    for widths in groups:
        left, left_got = refs[at : at + 2]
        at += 2
        for _ in widths:
            right, right_got = refs[at : at + 2]
            at += 2
            parts.append((dot_nn(left[...], right[...]) + dot_nn(left_got[...], right_got[...])).astype(BF16))
    if extra:
        parts.append((refs[at][...] + refs[at + 1][...]).astype(BF16))
        at += 2
    send, keep = refs[at:]
    g = parts[0] if len(parts) == 1 else jnp.concatenate(parts, axis=1)

    @pl.when(t < 2)
    def _():
        send[0] = g

    @pl.when(t >= 2)
    def _():
        keep[0] = g


def second_kernel(keep, got, out):
    out[...] = (keep[0].astype(F32) + got[0].astype(F32)).astype(BF16)


def third_kernel(size, band, keep, got, more, keep_o, send_o, held):
    held[...] = keep[0].astype(F32) + got[0].astype(F32) + more[...].astype(F32)
    for i in range(2):
        near = jnp.bitwise_xor(band[0], 2 * i)
        far = jnp.bitwise_xor(band[0], 2 * i + 1)
        keep_o[i] = held[pl.ds(pl.multiple_of(near * size, 8), size), :]
        send_o[i] = held[pl.ds(pl.multiple_of(far * size, 8), size), :].astype(BF16)


def last_kernel(widths, vectors, keep, got, more, *outs):
    at = 0
    for w, out in zip(widths, outs):
        cols = pl.ds(at, w)
        out[...] = keep[0, :, cols] + got[0, :, cols].astype(F32) + more[:, cols].astype(F32)
        at += w
    if vectors:
        cols = pl.ds(at, COLS)
        table = jnp.transpose(keep[0, :, cols] + got[0, :, cols].astype(F32) + more[:, cols].astype(F32))
        for (first, n), out in zip(vectors, outs[len(widths) :]):
            out[...] = jnp.concatenate([table[first + i : first + i + 1, :] for i in range(n)], axis=1)


COLS = 128
LIMIT = pltpu.CompilerParams(vmem_limit_bytes=20 * 1024 * 1024)
USED = (16, 17, 8, 9, 2, 0, 1, 3)


VM = pl.BlockSpec(memory_space=pltpu.VMEM)
SM = pl.BlockSpec(memory_space=pltpu.SMEM)


def shape(*dims, dtype=BF16):
    return jax.ShapeDtypeStruct(dims, dtype)


def cost(us):
    return pl.CostEstimate(flops=int(us * 2500000000), bytes_accessed=int(us * 10000000), transcendentals=0)


def after(x, *others):
    return lax.optimization_barrier((x, others))[0]


def scalar(x):
    return x.astype(jnp.int32).reshape(1)


class Links:
    def __init__(self, n_img, n_band):
        self.n_img, self.nb = n_img, n_band
        self.hi = n_img // 8
        i = lax.axis_index("img")
        self.c = i & 1
        self.p = (i >> 1) & 1
        self.q = (i >> 2) & 1
        self.h = i >> 3
        self.b = lax.axis_index("band")

    def flip(self, x, bit):
        return lax.ppermute(x, "img", [(k, k ^ bit) for k in range(self.n_img)])

    def flip_by_core(self, x, even, odd):
        return lax.ppermute(x, "img", [(k, k ^ (odd if k & 1 else even)) for k in range(self.n_img)])

    def flip_band(self, x, bit):
        return lax.ppermute(x, "band", [(k, k ^ bit) for k in range(self.nb)])

    def band_shift(self, x, s):
        return lax.ppermute(x, "band", [(k, (k + s) % self.nb) for k in range(self.nb)])

    def hi_shift(self, x, s):
        n = self.n_img
        return lax.ppermute(x, "img", [(k, (k + 8 * s) % n) for k in range(n)])

    def sum_hi(self, x):
        x = x.reshape(self.hi, x.shape[0] // self.hi, *x.shape[1:])
        total = take(x, self.h, 0)
        for s in range(1, self.hi):
            total = total + self.hi_shift(take(x, (self.h + s) % self.hi, 0).astype(BF16), s).astype(F32)
        return total

    def by_quarter(self, x):
        if self.hi == 1:
            return x
        return x.reshape(self.hi, 4, -1, x.shape[1]).swapaxes(0, 1).reshape(x.shape)

    def reclass(self, first, second, block):
        x = jnp.concatenate([first, second], axis=0)
        x = x.reshape(-1, 2, block, x.shape[1])
        own, other = take(x, self.c, 1), take(x, 1 - self.c, 1)
        return own.reshape(-1, x.shape[3]), other.reshape(-1, x.shape[3])


class Unit:
    def __init__(self, links, rows, groups, extra=()):
        self.links, self.vectors = links, []
        args, specs, widths = [], [], []
        tokens = groups[0][0].shape[1]
        self.block = block = rows // 4
        for left, left_got, left_at, rights in groups:
            if links.hi > 1:
                left, left_got = (x[left_at * rows : (left_at + 1) * rows, :] for x in (left, left_got))
                left_at = 0
            args += [links.by_quarter(left), links.by_quarter(left_got)]
            specs += [pl.BlockSpec((block, tokens), lambda t, s, i=4 * left_at: (s[t] + i, 0))] * 2
            widths.append([w for w, _, _, _, _ in rights])
            for w, own, own_at, got, got_at in rights:
                args += [own, got]
                specs.append(pl.BlockSpec((tokens, w), lambda t, s, i=own_at: (0, i)))
                specs.append(pl.BlockSpec((tokens, w), lambda t, s, i=got_at: (0, i)))
        for x in extra:
            args.append(links.by_quarter(x))
            specs.append(pl.BlockSpec((block, COLS), lambda t, s: (s[t], 0)))
        self.extra = len(extra) > 0
        self.widths = [w for ws in widths for w in ws] + [COLS] * self.extra
        self.cols = cols = sum(self.widths)
        p, q = links.p, links.q
        even = links.c == 0
        at = lambda a, b: a * 2 + b
        quarters = jnp.stack(
            [
                jnp.where(even, at(q, 1 - p), at(1 - q, p)), at(1 - q, 1 - p),
                jnp.where(even, at(1 - q, p), at(q, 1 - p)), at(q, p),
            ]
        ).astype(jnp.int32)
        one = lambda x: jnp.asarray(x).astype(jnp.int32)
        self.send, self.keep = pl.pallas_call(
            functools.partial(weight_kernel, widths, self.extra),
            grid_spec=pltpu.PrefetchScalarGridSpec(
                num_scalar_prefetch=1,
                grid=(4,),
                in_specs=specs,
                out_specs=[
                    pl.BlockSpec((1, block, cols), lambda t, s: (one(t > 0), 0, 0)),
                    pl.BlockSpec((1, block, cols), lambda t, s: (one(t < 3), 0, 0)),
                ],
            ),
            out_shape=[shape(2, block, cols)] * 2,
            cost_estimate=cost(0.1 if extra else 6),
            compiler_params=LIMIT,
            name="weight_grad",
        )(quarters, *args)
        self.got = links.flip_by_core(self.send, 2, 4)

    def pick(self, i):
        return pl.BlockSpec((1, self.block, self.cols), lambda _: (i, 0, 0))

    def whole(self, *dims):
        return pl.BlockSpec(dims, lambda _: (0,) * len(dims))

    def second(self, *deps):
        dims = (self.block, self.cols)
        sent = pl.pallas_call(
            second_kernel,
            grid=(1,),
            in_specs=[self.pick(1)] * 2,
            out_specs=self.whole(*dims),
            out_shape=shape(*dims),
            cost_estimate=cost(2),
            compiler_params=LIMIT,
            name="second",
        )(after(self.keep, *deps), self.got)
        self.more = self.links.flip_by_core(sent, 4, 2)
        return sent

    def third(self, *deps):
        links, nb, cols = self.links, self.links.nb, self.cols
        self.size = size = self.block // (links.hi * nb)
        keep = after(self.keep, *deps)
        if links.hi > 1 or size % 8:
            held = links.sum_hi(keep[0].astype(F32) + self.got[0].astype(F32) + self.more.astype(F32))
            held = held.reshape(nb, size, cols)
            piece = lambda bits: take(held, links.b ^ bits, 0)
            self.near = jnp.stack([piece(0), piece(2)])
            sent = jnp.stack([piece(1), piece(3)]).astype(BF16)
        else:
            self.near, sent = pl.pallas_call(
                functools.partial(third_kernel, size),
                grid=(1,),
                in_specs=[SM, self.pick(0), self.pick(0), self.whole(self.block, cols)],
                out_specs=[self.whole(2, size, cols)] * 2,
                out_shape=[shape(2, size, cols, dtype=F32), shape(2, size, cols)],
                scratch_shapes=[pltpu.VMEM((self.block, cols), F32)],
                cost_estimate=cost(3),
                compiler_params=LIMIT,
                name="third",
            )(scalar(links.b), keep, self.got, self.more)
        self.near_got = links.flip_band(sent, 1)
        return sent

    def fourth(self, *deps):
        dims = (self.size, self.cols)
        pick = pl.BlockSpec((1,) + dims, lambda _: (1, 0, 0))
        sent = pl.pallas_call(
            second_kernel,
            grid=(1,),
            in_specs=[pick] * 2,
            out_specs=self.whole(*dims),
            out_shape=shape(*dims),
            cost_estimate=cost(2),
            compiler_params=LIMIT,
            name="fourth",
        )(after(self.near, *deps), self.near_got)
        self.far_got = self.links.flip_band(sent, 2)
        return sent

    def last(self, *deps):
        dims = (self.size, self.cols)
        pick = pl.BlockSpec((1,) + dims, lambda _: (0, 0, 0))
        vectors = self.vectors
        outs = [(self.size, w) for w in self.widths] + [(1, n * self.size) for _, n in vectors]
        return pl.pallas_call(
            functools.partial(last_kernel, self.widths, vectors),
            grid=(1,),
            in_specs=[pick, pick, self.whole(*dims)],
            out_specs=[self.whole(*d) for d in outs],
            out_shape=[shape(*d, dtype=F32) for d in outs],
            cost_estimate=cost(2),
            compiler_params=LIMIT,
            name="last",
        )(after(self.near, *deps), self.near_got, self.far_got)


def per_device(
    inputs, keep_mask, crop_rows, crop_cols, gain_one, shift_one, w_query, b_query, w_key, w_value,
    b_value, w_out, b_out, gain_two, shift_two, w_up, b_up, w_down, b_down, cotangent, *, n_img, nb,
):
    images, rows, width = inputs.shape
    hidden_width = w_up.shape[1]
    assert images == nb and nb == 4
    tokens = nb * rows
    links = Links(n_img, nb)
    core, band = scalar(links.c), scalar(links.b)
    f = lambda v: v.astype(F32)

    blocks = pl.pallas_call(
        functools.partial(spread_kernel, rows, nb),
        in_specs=[SM] * 3 + [VM] * 2,
        out_specs=[VM] * nb,
        out_shape=[shape(rows + 8, width)] * nb,
        cost_estimate=cost(2),
        name="spread",
    )(band, crop_rows, crop_cols, inputs, keep_mask)
    slots = [blocks[0]] + [links.band_shift(blocks[s], s) for s in range(1, nb)]
    given = after(cotangent, *blocks)
    cots = [take(given, links.b, 0)]
    for s in range(1, nb):
        cots.append(links.band_shift(take(given, (links.b + s) % nb, 0), s))
    vec = jnp.stack([f(t) for t in (gain_one, shift_one, b_query, b_value, b_out, gain_two, shift_two, b_down)])
    b_up_row = f(b_up)[None, :]

    block = width // (links.hi * 8)
    aligned = block % 16 == 0
    up_block = hidden_width // (links.hi * 8)
    half = width // 2
    full = shape(tokens, width)
    left_keep, left_send, q, k, v, middle, two, mask = pl.pallas_call(
        functools.partial(attend_kernel, rows, nb, block if aligned else half),
        in_specs=[SM] + [VM] * (nb + 5),
        out_specs=[VM] * 8,
        out_shape=[shape(3 * half, tokens)] * 2 + [full] * 3
        + [shape(tokens, width, dtype=F32), full, shape(8, tokens, dtype=F32)],
        scratch_shapes=[pltpu.VMEM((tokens, width), BF16), pltpu.VMEM((width, tokens), BF16)],
        cost_estimate=cost(9),
        name="attend",
    )(core if aligned else jnp.zeros_like(core), *slots, vec, w_query, w_key, w_value, w_out)
    third_of = lambda x, i: x[i * half : (i + 1) * half, :]
    if not aligned:
        pairs = [links.reclass(third_of(left_keep, i), third_of(left_send, i), block) for i in range(3)]
        left_keep, left_send = (jnp.concatenate(x, axis=0) for x in zip(*pairs))
    left_got = links.flip(left_send, 1)

    steps = 4
    wide = hidden_width // steps
    fixed = lambda *dims: pl.BlockSpec(dims, lambda j, *_: (0,) * len(dims))
    tall = lambda *dims: pl.BlockSpec(dims, lambda j, *_: (0, j))
    up = pl.pallas_call(
        functools.partial(up_kernel, rows, nb, steps, up_block),
        grid_spec=pltpu.PrefetchScalarGridSpec(
            num_scalar_prefetch=1,
            grid=(steps,),
            in_specs=[
                fixed(tokens, width), fixed(tokens, width), fixed(8, tokens), fixed(8, width),
                tall(width, wide), tall(1, wide),
                pl.BlockSpec((wide, width), lambda j, c: (j, 0)),
            ] + [fixed(rows, width)] * nb,
            out_specs=[pl.BlockSpec((wide // 2, tokens), lambda j, c: (j, 0))] * 2
            + [fixed(tokens, width + hidden_width), tall(8, wide), fixed(tokens, width)],
            scratch_shapes=[pltpu.VMEM((tokens, width), F32)],
        ),
        out_shape=[shape(hidden_width // 2, tokens)] * 2
        + [shape(tokens, width + hidden_width), shape(8, hidden_width, dtype=F32), full],
        cost_estimate=cost(10),
        name="up",
    )(core, two, middle, mask, vec, w_up, b_up_row, w_down, *cots)
    act_keep, act_send, right, up_sums, result = up
    act_got = links.flip(act_send, 1)
    right_got = links.flip(right, 1)

    grad_middle, grad_branch, down_sums = pl.pallas_call(
        functools.partial(down_kernel, rows, nb, steps),
        grid=(steps,),
        in_specs=[
            fixed(tokens, width), pl.BlockSpec((tokens, wide), lambda j: (0, j + width // wide)), tall(width, wide),
            fixed(tokens, width), fixed(8, tokens), fixed(8, width),
        ] + [fixed(rows, width)] * nb,
        out_specs=[fixed(tokens, width), fixed(tokens, width), fixed(8, width)],
        out_shape=[shape(tokens, width, dtype=F32), full, shape(8, width, dtype=F32)],
        scratch_shapes=[pltpu.VMEM((tokens, width), F32)],
        cost_estimate=cost(7),
        name="down",
    )(right, right, w_up, after(middle, left_got), mask, vec, *cots)
    branch_got = links.flip(grad_branch, 1)

    unit_down = Unit(
        links, hidden_width // 2,
        [(after(act_keep, grad_branch), act_got, 0, [(width, right, 0, right_got, 0)])],
    )
    unit_up = Unit(
        links, half,
        [
            (
                after(left_keep, unit_down.send), left_got, 2,
                [(width, right, 1 + i, right_got, 1 + i) for i in range(hidden_width // width)],
            ),
            (left_keep, left_got, 1, [(width, grad_branch, 0, branch_got, 0)]),
        ],
    )
    low = lambda: pltpu.VMEM((width, tokens), BF16)
    back_right, attend_sums = pl.pallas_call(
        attend_back_kernel,
        in_specs=[VM] * 6,
        out_specs=[VM] * 2,
        out_shape=[shape(tokens, 3 * width), shape(8, width, dtype=F32)],
        scratch_shapes=[
            pltpu.VMEM((tokens, width), BF16), pltpu.VMEM((tokens, width), BF16), low(), low(), low(), low(),
            pltpu.VMEM((width, tokens), F32), pltpu.VMEM((width, tokens), F32),
        ],
        cost_estimate=cost(11),
        compiler_params=LIMIT,
        name="attend_back",
    )(after(grad_branch, unit_up.send), q, k, v, mask, w_out)
    back_got = links.flip(back_right, 1)

    results = pl.pallas_call(
        functools.partial(by_band, rows, nb),
        in_specs=[SM, VM],
        out_specs=[VM] * 3,
        out_shape=[shape(rows, width), shape(2 * rows, width), shape(rows, width)],
        cost_estimate=cost(1),
        compiler_params=LIMIT,
        name="by_band",
    )(band, after(result, unit_up.send))
    result_near = links.flip_band(results[1], 1)
    mark = unit_down.second(back_right)
    per_row = hidden_width // width
    up_cols = after(up_sums, unit_down.send)[0].reshape(n_img * nb, per_row, -1).swapaxes(1, 2).reshape(width, per_row)
    up_cols = jnp.pad(up_cols, ((0, 0), (18, COLS - 18 - per_row)))
    back = pl.pallas_call(
        functools.partial(input_back_kernel, rows, nb, block if aligned else half),
        in_specs=[SM] * 2 + [VM] * (nb + 9),
        out_specs=[VM] * 5,
        out_shape=[shape(rows, width), shape(2 * rows, width), shape(rows, width)]
        + [shape(half, COLS, dtype=F32)] * 2,
        scratch_shapes=[pltpu.VMEM((tokens, width), BF16)],
        cost_estimate=cost(5),
        compiler_params=LIMIT,
        name="input_back",
    )(
        core if aligned else jnp.zeros_like(core), band,
        *slots, after(back_right, mark), w_query, w_key, w_value, grad_middle, vec, down_sums, attend_sums, up_cols,
    )
    blocks, table = back[:3], back[3:]
    near_got = links.flip_band(blocks[1], 1)
    if not aligned:
        table = links.reclass(*table, block)
    table_got = links.flip(table[1], 1)

    unit_qkv = Unit(
        links, half,
        [(after(left_keep, blocks[0]), left_got, 0, [(width, back_right, i, back_got, i) for i in range(3)])],
        (table[0], table_got),
    )
    result_far = links.flip_band(jnp.concatenate([after(results[2], blocks[0]), result_near[rows:, :]]), 2)
    far_got = links.flip_band(jnp.concatenate([after(blocks[2], unit_qkv.send), near_got[rows:, :]]), 2)
    mark = unit_up.second(unit_qkv.send)
    mark = unit_down.third(mark)
    mark = unit_qkv.second(mark)
    mark = unit_up.third(mark)
    mark = unit_down.fourth(mark)
    mark = unit_qkv.third(mark)
    mark = unit_up.fourth(mark)
    mark = unit_qkv.fourth(mark)
    (g_w_down,) = unit_down.last(mark)
    output, grad_inputs = pl.pallas_call(
        gather_kernel,
        in_specs=[SM] + [VM] * 6,
        out_specs=[VM] * 2,
        out_shape=[shape(nb, rows, width), shape(nb, rows, width, dtype=F32)],
        cost_estimate=cost(2),
        compiler_params=LIMIT,
        name="gather",
    )(after(band, g_w_down), results[0], result_near, result_far, blocks[0], near_got, far_got)
    mark = output
    unit_up.widths = [hidden_width, width]
    g_w_up, g_w_out = unit_up.last(mark)
    if unit_qkv.size % 8 == 0:
        unit_qkv.widths = [width] * 3
        unit_qkv.vectors = [(i, 1) for i in USED] + [(18, per_row)]
        g_w_query, g_w_key, g_w_value, *rest = unit_qkv.last(g_w_up)
        sums = {i: x[0] for i, x in zip(USED + (18,), rest)}
    else:
        g_w_query, g_w_key, g_w_value, cols = unit_qkv.last(g_w_up)
        sums = [cols[:, i] for i in range(18)] + [cols[:, 18 : 18 + per_row].swapaxes(0, 1).reshape(-1)]
    return (
        output,
        grad_inputs,
        sums[16],
        sums[17],
        g_w_query,
        sums[8],
        g_w_key,
        g_w_value,
        sums[9],
        g_w_out,
        sums[2],
        sums[0],
        sums[1],
        g_w_up,
        sums[18],
        g_w_down,
        sums[3],
    )


def solution(mesh):
    n_img, nb = mesh.shape["img"], mesh.shape["band"]

    def body(*args):
        return per_device(*args, n_img=n_img, nb=nb)

    both = P(("img", "band"))
    rows = P(("img", "band"), None)
    token = P("img", "band", None)
    return jax.shard_map(
        body,
        mesh=mesh,
        in_specs=(token, P("img", "band"), P("img"), P("img")) + (P(),) * 15 + (token,),
        out_specs=(
            token, token, both, both, rows, both, rows, rows, both, rows, both, both, both, rows, both,
            rows, both,
        ),
        check_vma=False,
    )
```
